512 devices in a mesh: seq: 32 (over z, core), head: 16 (over y, x).
Axes of the slice: x: 4, y: 4, z: 16, core: 2. Of those that a mesh axis runs over, the one named last changes fastest.
Arguments:
- queries: bfloat16 [32768, 2048], P('seq', 'head'), may hold values from -1.5 to 1.5
- keys: bfloat16 [32768, 2048], P('seq', 'head'), may hold values from -1.5 to 1.5
- values: bfloat16 [32768, 2048], P('seq', 'head'), may hold values from -6 to 6
- log_decay: float32 [16, 32768], P('head', 'seq'), may hold values from -2 to 0, as said below
- out_weight: bfloat16 [2048, 2048], P(None, 'head'), may hold values from -0.125 to 0.125
- out_grad: bfloat16 [32768, 2048], P('seq', 'head'), may hold values from -0.75 to 0.75
Outputs:
- attended: bfloat16 [32768, 2048], P('seq', 'head')
- query_grad: bfloat16 [32768, 2048], P('seq', 'head')
- key_grad: bfloat16 [32768, 2048], P('seq', 'head')
- value_grad: bfloat16 [32768, 2048], P('seq', 'head')
- weight_grad: bfloat16 [2048, 2048], P('seq', 'head')
The draws below stay inside these ranges and needn't reach their ends.
Inputs may be any that keep to these rules, and one draw needn't show every extreme that they name: `log_decay`: natural logarithm of the factor by which a head's state is multiplied before the token's own key and value are added; always negative.
All inputs are finite; a program needn't handle non-finite values.
Results may differ from the reference program's by a relative error of at most 0.0069.
Values may be sent and summed in bfloat16 or wider, within the bound.
A program may use at most 64 MiB of HBM per device.

```python
import math
import jax
import jax.numpy as jnp
from jax import lax

D = 2048
HEAD_COUNT = 16
DH = 128
TOK_DEV = 1024
SEQUENCE_TOKENS = 32768


def draw_log_decay(key, part):
    category_key, seed_key, block_random_key, jagged_random_key, location_key, spike_random_key = jax.random.split(key, 6)
    kinds = jax.random.randint(category_key, (HEAD_COUNT, 1), 0, 4)
    jagged_decay = jax.random.uniform(jagged_random_key, (HEAD_COUNT, SEQUENCE_TOKENS), jnp.float32, 0.4, 1.6)
    picker = jax.random.uniform(seed_key, (HEAD_COUNT, 1), jnp.float32, 0.0, 1.0)
    fast_rate = jnp.exp(math.log(1.0 / 50.0) + picker * math.log(50.0 / 30.0))
    middle_rate = (1.0 + 3.0 * picker) / TOK_DEV
    slow_rate = (0.2 + 0.6 * picker) / SEQUENCE_TOKENS
    decay_speed = jnp.where(kinds == 0, fast_rate, jnp.where(kinds == 1, middle_rate, slow_rate))
    block_count = SEQUENCE_TOKENS // TOK_DEV
    block_multiplier = jnp.exp(jax.random.uniform(block_random_key, (HEAD_COUNT, block_count), jnp.float32, -math.log(2.0), math.log(2.0)))
    block_multiplier = jnp.repeat(block_multiplier, TOK_DEV, axis=1)
    spots = jax.random.randint(location_key, (HEAD_COUNT, 3), 0, SEQUENCE_TOKENS)
    places = jnp.arange(SEQUENCE_TOKENS, dtype=jnp.int32)
    spike_positions = jnp.sum((places[None, None, :] == spots[:, :, None]).astype(jnp.float32), axis=1)
    spike_tokens = jax.random.uniform(spike_random_key, (HEAD_COUNT, SEQUENCE_TOKENS), jnp.float32, math.log(0.65), math.log(0.8))
    return (-decay_speed * block_multiplier * jagged_decay + spike_positions * spike_tokens).astype(jnp.float32)


def spiked(values, stream_key, source, target, blocks, factor):
    def block_of(position):
        return (jnp.arange(values.shape[position]) // (values.shape[position] // blocks)).reshape((-1,) + (1,) * (values.ndim - 1 - position))

    first = jax.random.permutation(stream_key, blocks)[block_of(target)]
    other_side = (block_of(target) + blocks // 2) % blocks
    return jnp.where((block_of(source) == first) | (block_of(source) == other_side), factor * values, values)


def block_levels(key, dims, pieces, least, top_value):
    gain, own = 1.0, jax.random.fold_in(key, 6)
    for axis_at, parts in pieces:
        heights = jnp.exp(jax.random.uniform(jax.random.fold_in(own, axis_at), (parts,), jnp.float32, least / len(pieces), top_value / len(pieces)))
        gain = gain * jnp.repeat(heights, dims[axis_at] // parts).reshape([-1 if axis == axis_at else 1 for axis in range(len(dims))])
    return gain


def gaussian(rng, extent, scale, bound, cuts=(), held_as=jnp.bfloat16):
    values = scale * jax.random.normal(rng, extent, jnp.float32)
    if cuts:
        values = values * block_levels(rng, extent, cuts, -0.22, 0.18)
    return jnp.clip(values, -bound, bound).astype(held_as)


def heavy_noise(stream_key, dims, width, limit, pieces, heavy, kind=jnp.bfloat16):
    values = width * jax.random.normal(stream_key, dims, jnp.float32)
    if pieces:
        values = values * block_levels(stream_key, dims, pieces, -0.22, 0.18)
    return jnp.clip(spiked(values, jax.random.fold_in(stream_key, 3), *heavy), -limit, limit).astype(kind)


def setup_inputs(seed: int = 0) -> dict:
    arg_keys = jax.random.split(jax.random.key(seed), 7)
    return {
        "queries": gaussian(arg_keys[0], (SEQUENCE_TOKENS, HEAD_COUNT * DH), 0.25, 1.5, ((0, 32), (1, 16))),
        "keys": gaussian(arg_keys[1], (SEQUENCE_TOKENS, HEAD_COUNT * DH), 0.25, 1.5, ((0, 32), (1, 16))),
        "values": gaussian(arg_keys[2], (SEQUENCE_TOKENS, HEAD_COUNT * DH), 1.0, 6.0, ((0, 32), (1, 16))),
        "log_decay": draw_log_decay(jax.random.fold_in(arg_keys[6], 71), 0),
        "out_weight": gaussian(arg_keys[4], (D, HEAD_COUNT * DH), (HEAD_COUNT * DH) ** -0.5, 0.125, ((1, 16),)),
        "out_grad": heavy_noise(arg_keys[5], (SEQUENCE_TOKENS, D), 0.125, 0.75, ((0, 32), (1, 16)), (0, 1, 32, 2.75)),
    }


HIGH = lax.Precision.HIGHEST

def to_low(array):
    return lax.optimization_barrier(array.astype(jnp.bfloat16)).astype(jnp.float32)

def one_head(inputs):
    query_rows, key_rows, value_rows, decay_rows, head_grad = inputs
    length = query_rows.shape[1]
    running = jnp.cumsum(decay_rows, axis=1)
    totals = running[:, -1]
    row_index = lax.broadcasted_iota(jnp.int32, (length, length), 0)
    col_index = lax.broadcasted_iota(jnp.int32, (length, length), 1)
    causal = (row_index >= col_index)[None]
    spread = running[:, :, None] - running[:, None, :]
    decay = jnp.where(causal, jnp.exp(jnp.where(causal, spread, 0.0)), 0.0)
    query_wide = query_rows.astype(jnp.float32)
    key_wide = key_rows.astype(jnp.float32)
    value_wide = value_rows.astype(jnp.float32)
    scores = jnp.einsum('ntd,nsd->nts', query_wide, key_wide, precision=HIGH)
    weights = (scores * decay).astype(jnp.bfloat16)
    tail_decay = jnp.exp(totals[:, None] - running)
    growth = jnp.exp(running)
    key_tail = to_low(key_wide * tail_decay[:, :, None])
    value_tail = to_low(value_wide * tail_decay[:, :, None])
    query_grown = to_low(query_wide * growth[:, :, None])
    update = jnp.einsum('nsd,nse->nde', key_tail, value_wide, precision=HIGH)

    def forward_step(state, item):
        total_now, block_state = item
        return (jnp.exp(total_now) * state + block_state, state)
    start_state = jnp.zeros(update.shape[1:], jnp.float32)
    _, incoming = lax.scan(forward_step, start_state, (totals, update))
    incoming_low = to_low(incoming)
    local_part = jnp.einsum('nts,nse->nte', weights.astype(jnp.float32), value_wide, precision=HIGH)
    carried = jnp.einsum('ntd,nde->nte', query_grown, incoming_low, precision=HIGH)
    mixed = local_part + carried
    root_mean = jnp.sqrt(lax.optimization_barrier(jnp.mean(mixed * mixed, axis=2, keepdims=True)) + 1e-05)
    normed = mixed / root_mean
    attended = normed.astype(jnp.bfloat16)
    norm_grad = (head_grad - normed * lax.optimization_barrier(jnp.mean(head_grad * normed, axis=2, keepdims=True))) / root_mean
    mixed_grad = norm_grad.astype(jnp.bfloat16)
    grad_wide = mixed_grad.astype(jnp.float32)
    grad_grown = to_low(grad_wide * growth[:, :, None])
    pair_grad = jnp.einsum('ntd,nsd->nts', grad_wide, value_wide, precision=HIGH)
    masked_grad = (pair_grad * decay).astype(jnp.bfloat16)
    back_update = jnp.einsum('ntd,nte->nde', query_grown, grad_wide, precision=HIGH)

    def backward_step(state, item):
        total_now, block_state = item
        return (block_state + jnp.exp(total_now) * state, state)
    _, outgoing = lax.scan(backward_step, start_state, (totals, back_update), reverse=True)
    outgoing_low = to_low(outgoing)
    masked_wide = masked_grad.astype(jnp.float32)
    weights_wide = weights.astype(jnp.float32)
    query_grad = jnp.einsum('nts,nsd->ntd', masked_wide, key_wide, precision=HIGH) + jnp.einsum('nte,nde->ntd', grad_grown, incoming_low, precision=HIGH)
    key_grad = jnp.einsum('nts,ntd->nsd', masked_wide, query_wide, precision=HIGH) + jnp.einsum('nse,nde->nsd', value_tail, outgoing_low, precision=HIGH)
    value_grad = jnp.einsum('nts,nte->nse', weights_wide, grad_wide, precision=HIGH) + jnp.einsum('nsd,nde->nse', key_tail, outgoing_low, precision=HIGH)
    return (attended, query_grad.astype(jnp.bfloat16), key_grad.astype(jnp.bfloat16), value_grad.astype(jnp.bfloat16))

def reference(queries, keys, values, log_decay, out_weight, out_grad):
    blocks = SEQUENCE_TOKENS // TOK_DEV

    def split_heads(array):
        return array.reshape(blocks, TOK_DEV, HEAD_COUNT, DH).transpose(2, 0, 1, 3)

    def join_heads(array):
        return array.transpose(1, 2, 0, 3).reshape(SEQUENCE_TOKENS, HEAD_COUNT * DH)
    head_grad = jnp.dot(out_grad, out_weight, preferred_element_type=jnp.float32)
    stacked = (split_heads(queries), split_heads(keys), split_heads(values), log_decay.reshape(HEAD_COUNT, blocks, TOK_DEV), split_heads(head_grad))
    results = lax.map(one_head, stacked)
    attended = join_heads(results[0])
    query_grad = join_heads(results[1])
    key_grad = join_heads(results[2])
    value_grad = join_heads(results[3])
    weight_grad = jnp.dot(out_grad.T, attended, preferred_element_type=jnp.float32).astype(jnp.bfloat16)
    return (attended, query_grad, key_grad, value_grad, weight_grad)
```

```python
import functools

import jax
import jax.numpy as jnp
from jax import lax
from jax.experimental import pallas as pl
from jax.experimental.pallas import tpu as pltpu
from jax.sharding import PartitionSpec as P

MESH = pl.DeviceIdType.MESH
F32 = jnp.float32
BF16 = jnp.bfloat16
GROUPS = 4
INNER = 8
RING = 4
TILE = 256
DH = 128


def dot(a, b, ca=1, cb=0):
    return lax.dot_general(a, b, (((ca,), (cb,)), ((), ())), preferred_element_type=F32)


def kernel(
    q_ref, k_ref, v_ref, ld_ref, ow_ref, og_ref,
    att_ref, qg_ref, kg_ref, vg_ref, wg_ref,
    full, run_col, run_row, qgrow, ktail, vtail, weights, decay, masked, mixed, mg,
    kacc, vacc, upd, got, tots, gsum, gtot, inc_out, inc,
    bupd, bgot, bsum, out_out, outg, dw, dwgot, dwsum, dwfin,
    g_s, g_r, t_s, t_r, r1_s, r1_r, r2_s, r2_r, r2t_s, r2t_r, r3_s, r3_r,
    b1_s, b1_r, b2_s, b2_r, b3_s, b3_r, w1_s, w1_r, w2_s, w2_r,
):
    tokens = q_ref.shape[0]
    half, quarter = tokens // 2, tokens // 4
    s = lax.axis_index("seq")
    h = lax.axis_index("head")
    g, j = s // INNER, s % INNER
    y, x = h // RING, h % RING

    def head_at(dy, dx):
        return ((y + dy + RING) % RING) * RING + (x + dx + RING) % RING

    inner_peers = [(j + k) % INNER for k in range(1, INNER)]
    outer_peers = [(g + k) % GROUPS for k in range(1, GROUPS)]

    barrier = pltpu.get_barrier_semaphore()
    for dy, dx in ((0, 1), (0, -1), (1, 0), (-1, 0)):
        pl.semaphore_signal(barrier, inc=1, device_id=(s, head_at(dy, dx)), device_id_type=MESH)
    for p in inner_peers:
        pl.semaphore_signal(barrier, inc=1, device_id=(g * INNER + p, h), device_id_type=MESH)
    for p in outer_peers:
        pl.semaphore_signal(barrier, inc=1, device_id=(p * INNER + j, h), device_id_type=MESH)

    lane = lax.broadcasted_iota(jnp.int32, (DH, DH), 1)
    row = lax.broadcasted_iota(jnp.int32, (DH, DH), 0)
    lower = lane <= row
    offset = jnp.zeros((1, 1), F32)
    for n in range(tokens // DH):
        piece = jnp.broadcast_to(ld_ref[:, n * DH : (n + 1) * DH], (DH, DH))
        col = jnp.sum(jnp.where(lower, piece, 0.0), axis=1, keepdims=True) + offset
        offset = col[DH - 1 : DH, :]
        wide = jnp.broadcast_to(col, (DH, DH))
        run_col[n * DH : (n + 1) * DH, :] = wide
        run_row[:, n * DH : (n + 1) * DH] = wide.T[0:8, :]
    total = jnp.broadcast_to(offset, (1, DH))
    tots[j] = total

    rc = run_col[...]
    tail = jnp.exp(total - rc)
    kt = (k_ref[...].astype(F32) * tail).astype(BF16)
    ktail[...] = kt
    update = dot(kt, v_ref[...], 0, 0).astype(BF16).reshape(INNER, DH // INNER, DH)
    upd[...] = update
    got[j] = upd[j]
    vtail[...] = (v_ref[...].astype(F32) * tail).astype(BF16)
    qgrow[...] = (q_ref[...].astype(F32) * jnp.exp(rc)).astype(BF16)
    full[h] = og_ref[...]

    pl.semaphore_wait(barrier, 4 + (INNER - 1) + (GROUPS - 1))

    gather = {}
    started = []

    def send(name, src, block, first, count, dy, dx):
        n = len(gather)
        rows = pl.ds(first, count)
        copy = pltpu.make_async_remote_copy(
            src_ref=src.at[rows] if src is not None else full.at[block, rows],
            dst_ref=full.at[block, rows],
            send_sem=g_s.at[n],
            recv_sem=g_r.at[n],
            device_id=(s, head_at(dy, dx)),
            device_id_type=MESH,
        )
        copy.start()
        gather[name] = copy
        started.append(copy)

    def step(kind, first, second):
        return (second, first) if kind == "A" else (first, second)

    def block_of(kind, first, second):
        dy, dx = step(kind, first, second)
        return head_at(dy, dx)

    base = {"A": 0, "B": half}

    def stage0():
        for kind, axis in (("A", 0), ("B", 0), ("B", 1), ("A", 1)):
            for sign in (1, -1):
                dy, dx = step(kind, sign, 0) if axis == 0 else step(kind, 0, sign)
                send((kind, axis, 0, sign), og_ref, h, base[kind], half, dy, dx)

    def arrived(*name):
        gather[name].wait_recv()

    def relay(kind, axis, name, other):
        for sign in (1, -1):
            dy, dx = step(kind, sign, 0) if axis == 0 else step(kind, 0, sign)
            blk = block_of(kind, -sign, 0) if axis == 0 else block_of(kind, other, -sign)
            part = base[kind] + (0 if sign == 1 else quarter)
            send((kind, axis, name, sign, "far"), None, blk, part, quarter, dy, dx)

    def turn(kind, offsets):
        for off in offsets:
            for sign in (1, -1):
                dy, dx = step(kind, 0, sign)
                send((kind, 1, off, sign), None, block_of(kind, off, 0), base[kind], half, dy, dx)

    def stage1():
        for kind in "AB":
            arrived(kind, 0, 0, 1)
            arrived(kind, 0, 0, -1)
            relay(kind, 0, 0, 0)
            turn(kind, (-1, 1))

    def stage2():
        for kind in "AB":
            arrived(kind, 1, 0, 1)
            arrived(kind, 1, 0, -1)
            relay(kind, 1, 0, 0)

    def stage3():
        for kind in "AB":
            arrived(kind, 0, 0, 1, "far")
            arrived(kind, 0, 0, -1, "far")
            turn(kind, (2,))

    def stage4():
        for kind in "AB":
            for off in (-1, 1):
                arrived(kind, 1, off, 1)
                arrived(kind, 1, off, -1)
                relay(kind, 1, off, off)

    def stage5():
        for kind in "AB":
            arrived(kind, 1, 2, 1)
            arrived(kind, 1, 2, -1)
            relay(kind, 1, 2, 2)

    def stage6():
        for kind in "AB":
            for off in (0, -1, 1, 2):
                arrived(kind, 1, off, 1, "far")
                arrived(kind, 1, off, -1, "far")

    def to_inner(src, dst, send_sem, recv_sem):
        out = []
        for k in range(1, INNER):
            p = inner_peers[k - 1]
            copy = pltpu.make_async_remote_copy(
                src_ref=src.at[p] if src is not None else dst.at[j],
                dst_ref=dst.at[j],
                send_sem=send_sem.at[k],
                recv_sem=recv_sem.at[k],
                device_id=(g * INNER + p, h),
                device_id_type=MESH,
            )
            copy.start()
            out.append(copy)
        started.extend(out)
        return out

    def to_outer(src, dst, send_sem, recv_sem):
        out = []
        for k in range(1, GROUPS):
            p = outer_peers[k - 1]
            copy = pltpu.make_async_remote_copy(
                src_ref=src.at[p] if src is not None else dst.at[g],
                dst_ref=dst.at[g],
                send_sem=send_sem.at[k],
                recv_sem=recv_sem.at[k],
                device_id=(p * INNER + j, h),
                device_id_type=MESH,
            )
            copy.start()
            out.append(copy)
        started.extend(out)
        return out

    def land(copies):
        for copy in copies:
            copy.wait_recv()

    totals_in = to_inner(None, tots, t_s, t_r)
    round1 = to_inner(upd, got, r1_s, r1_r)
    stage0()

    trow = lax.broadcasted_iota(jnp.int32, (TILE, TILE), 0)
    tcol = lax.broadcasted_iota(jnp.int32, (TILE, TILE), 1)
    causal = trow >= tcol

    def local(t):
        here = slice(t * TILE, (t + 1) * TILE)
        q = q_ref[here, :]
        here_run = run_col[here, 0:1]
        for u in range(t + 1):
            there = slice(u * TILE, (u + 1) * TILE)
            spread = here_run - run_row[0:1, there]
            if u == t:
                fade = jnp.where(causal, jnp.exp(jnp.where(causal, spread, 0.0)), 0.0)
            else:
                fade = jnp.exp(spread)
            decay[here, there] = fade
            score = dot(q, k_ref[there, :], 1, 1)
            weights[here, there] = (score * fade).astype(BF16)
        n = (t + 1) * TILE
        mixed[here, :] = dot(weights[here, :n], v_ref[:n, :])

    local(0)
    local(1)
    stage1()

    land(totals_in)
    land(round1)
    tot = [tots[n] for n in range(INNER)]
    grow = [jnp.exp(t) for t in tot]
    state = jnp.zeros((DH // INNER, DH), F32)
    before = []
    for n in range(INNER):
        before.append(state)
        state = grow[n] * state + got[n].astype(F32)
    gsum[g] = state
    lead = [jnp.zeros((1, DH), F32)]
    for n in range(INNER):
        lead.append(lead[-1] + tot[n])
    gtot[g] = lead[-1]
    round2 = to_outer(None, gsum, r2_s, r2_r)
    round2t = to_outer(None, gtot, r2t_s, r2t_r)

    local(2)
    stage2()
    local(3)
    stage3()

    land(round2)
    land(round2t)
    carried = jnp.zeros((DH // INNER, DH), F32)
    for n in range(GROUPS):
        carried = jnp.where(n < g, jnp.exp(gtot[n]) * carried + gsum[n], carried)
    for n in range(INNER):
        inc_out[n] = (jnp.exp(lead[n]) * carried + before[n]).astype(BF16)
    inc[j] = inc_out[j]
    round3 = to_inner(inc_out, inc, r3_s, r3_r)

    stage4()
    land(round3)
    incoming = inc[...].reshape(DH, DH)
    whole = mixed[...] + dot(qgrow[...], incoming)
    inv = lax.rsqrt(jnp.mean(whole * whole, axis=1, keepdims=True) + 1e-05)
    normed = whole * inv
    att = normed.astype(BF16)
    att_ref[...] = att
    mixed[...] = normed
    att_t = att.T

    stage5()
    stage6()

    head_grad = jnp.zeros((tokens, DH), F32)
    for n in range(0, RING * RING, 2):
        pair = jnp.concatenate([full[n], full[n + 1]], axis=1)
        head_grad = head_grad + dot(pair, ow_ref[n * DH : (n + 2) * DH, :])
    normed = mixed[...]
    grad = (head_grad - normed * jnp.mean(head_grad * normed, axis=1, keepdims=True)) * inv
    mgrad = grad.astype(BF16)
    mg[...] = mgrad
    bupd[...] = dot(qgrow[...], mgrad, 0, 0).astype(BF16).reshape(INNER, DH // INNER, DH)
    bgot[j] = bupd[j]
    back1 = to_inner(bupd, bgot, b1_s, b1_r)

    weight_in = []
    for c in range(GROUPS):
        for i in range(RING):
            n = c * RING + i
            rows = dot(att_t, full[n]).T.astype(BF16)
            dw[2 * i, c] = rows[: DH // 2, :]
            dw[2 * i + 1, c] = rows[DH // 2 :, :]
        for k in range(1, INNER):
            p = inner_peers[k - 1]
            copy = pltpu.make_async_remote_copy(
                src_ref=dw.at[p, c],
                dst_ref=dwgot.at[j, c],
                send_sem=w1_s.at[k, c],
                recv_sem=w1_r.at[k, c],
                device_id=(g * INNER + p, h),
                device_id_type=MESH,
            )
            copy.start()
            weight_in.append(copy)
    started.extend(weight_in)
    dwgot[j] = dw[j]

    land(back1)
    state = jnp.zeros((DH // INNER, DH), F32)
    after = [None] * INNER
    for n in reversed(range(INNER)):
        after[n] = state
        state = bgot[n].astype(F32) + grow[n] * state
    bsum[g] = state
    back2 = to_outer(None, bsum, b2_s, b2_r)

    def grads(t):
        here = slice(t * TILE, (t + 1) * TILE)
        n = (t + 1) * TILE
        pair = dot(mg[here, :], v_ref[:n, :], 1, 1)
        masked[here, :n] = (pair * decay[here, :n]).astype(BF16)
        own = dot(masked[here, :n], k_ref[:n, :])
        grown = (mg[here, :].astype(F32) * jnp.exp(run_col[here, :])).astype(BF16)
        qg_ref[here, :] = (own + dot(grown, incoming, 1, 1)).astype(BF16)

    grads(0)
    grads(1)
    grads(2)
    grads(3)

    land(back2)
    trail = [None] * INNER
    ahead = jnp.zeros((1, DH), F32)
    for n in reversed(range(INNER)):
        trail[n] = ahead
        ahead = ahead + tot[n]
    carried = jnp.zeros((DH // INNER, DH), F32)
    for n in reversed(range(GROUPS)):
        carried = jnp.where(n > g, bsum[n] + jnp.exp(gtot[n]) * carried, carried)
    for n in range(INNER):
        out_out[n] = (after[n] + jnp.exp(trail[n]) * carried).astype(BF16)
    outg[j] = out_out[j]
    back3 = to_inner(out_out, outg, b3_s, b3_r)

    land(weight_in)
    for c in range(GROUPS):
        acc = dwgot[0, c].astype(F32)
        for n in range(1, INNER):
            acc = acc + dwgot[n, c].astype(F32)
        dwsum[c] = acc.astype(BF16)
    dwfin[g] = dwsum[g]
    weight2 = to_outer(dwsum, dwfin, w2_s, w2_r)

    for u in range(tokens // TILE):
        there = slice(u * TILE, (u + 1) * TILE)
        m = u * TILE
        kacc[there, :] = dot(masked[m:, there], q_ref[m:, :], 0, 0)
        vacc[there, :] = dot(weights[m:, there], mg[m:, :], 0, 0)

    land(back3)
    outgoing = outg[...].reshape(DH, DH)
    kg_ref[...] = (kacc[...] + dot(vtail[...], outgoing, 1, 1)).astype(BF16)
    vg_ref[...] = (vacc[...] + dot(ktail[...], outgoing)).astype(BF16)

    land(weight2)
    acc = dwfin[0].astype(F32)
    for n in range(1, GROUPS):
        acc = acc + dwfin[n].astype(F32)
    wg_ref[...] = acc.astype(BF16)

    for copy in started:
        copy.wait_send()


def on_device(queries, keys, values, log_decay, out_weight, out_grad):
    tokens = queries.shape[0]
    piece = DH // INNER
    vmem = pl.BlockSpec(memory_space=pltpu.VMEM)
    block = jax.ShapeDtypeStruct((tokens, DH), BF16)
    rows = out_weight.shape[0] // (GROUPS * INNER)
    dma = pltpu.SemaphoreType.DMA
    inner, outer = dma((INNER,)), dma((GROUPS,))
    scratch = [
        pltpu.VMEM((RING * RING, tokens, DH), BF16),
        pltpu.VMEM((tokens, DH), F32),
        pltpu.VMEM((8, tokens), F32),
        pltpu.VMEM((tokens, DH), BF16),
        pltpu.VMEM((tokens, DH), BF16),
        pltpu.VMEM((tokens, DH), BF16),
        pltpu.VMEM((tokens, tokens), BF16),
        pltpu.VMEM((tokens, tokens), F32),
        pltpu.VMEM((tokens, tokens), BF16),
        pltpu.VMEM((tokens, DH), F32),
        pltpu.VMEM((tokens, DH), BF16),
        pltpu.VMEM((tokens, DH), F32),
        pltpu.VMEM((tokens, DH), F32),
        pltpu.VMEM((INNER, piece, DH), BF16),
        pltpu.VMEM((INNER, piece, DH), BF16),
        pltpu.VMEM((INNER, 1, DH), F32),
        pltpu.VMEM((GROUPS, piece, DH), F32),
        pltpu.VMEM((GROUPS, 1, DH), F32),
        pltpu.VMEM((INNER, piece, DH), BF16),
        pltpu.VMEM((INNER, piece, DH), BF16),
        pltpu.VMEM((INNER, piece, DH), BF16),
        pltpu.VMEM((INNER, piece, DH), BF16),
        pltpu.VMEM((GROUPS, piece, DH), F32),
        pltpu.VMEM((INNER, piece, DH), BF16),
        pltpu.VMEM((INNER, piece, DH), BF16),
        pltpu.VMEM((INNER, GROUPS, rows, DH), BF16),
        pltpu.VMEM((INNER, GROUPS, rows, DH), BF16),
        pltpu.VMEM((GROUPS, rows, DH), BF16),
        pltpu.VMEM((GROUPS, rows, DH), BF16),
        dma((40,)), dma((40,)),
        inner, inner,
        inner, inner, outer, outer, outer, outer, inner, inner,
        inner, inner, outer, outer, inner, inner,
        dma((INNER, GROUPS)), dma((INNER, GROUPS)), outer, outer,
    ]
    return pl.pallas_call(
        kernel,
        out_shape=(block, block, block, block, jax.ShapeDtypeStruct((rows, DH), BF16)),
        in_specs=[vmem] * 6,
        out_specs=(vmem,) * 5,
        scratch_shapes=scratch,
        compiler_params=pltpu.CompilerParams(collective_id=0, has_side_effects=True),
    )(queries, keys, values, log_decay, out_weight, out_grad)


def solution(mesh):
    return jax.shard_map(
        on_device,
        mesh=mesh,
        in_specs=(
            P("seq", "head"),
            P("seq", "head"),
            P("seq", "head"),
            P("head", "seq"),
            P(None, "head"),
            P("seq", "head"),
        ),
        out_specs=(P("seq", "head"),) * 5,
        check_vma=False,
    )
```

```python
import jax
import jax.numpy as jnp
from jax import lax
from jax.experimental import pallas as pl
from jax.experimental.pallas import tpu as pltpu
from jax.sharding import PartitionSpec as P

MESH = pl.DeviceIdType.MESH
F32 = jnp.float32
BF16 = jnp.bfloat16
GROUPS = 4
INNER = 8
CHIPS = 16
RING = 4
TILE = 256
DH = 128
PIECE = DH // INNER
BATCHES = ((0, 3), (3, 6), (6, 9), (9, 12), (12, 16))


def dot(a, b, ca=1, cb=0):
    return lax.dot_general(a, b, (((ca,), (cb,)), ((), ())), preferred_element_type=F32)


def kernel(
    q_hbm, k_hbm, v_hbm, ld_hbm, ow_hbm, og_hbm,
    att_ref, qg_ref, kg_ref, vg_ref, wg_ref,
    q_ref, k_ref, v_ref, ld_ref, ow_ref,
    full, run_col, run_row, qgrow, ktail, vtail, weights, decay, masked, mixed, scale, mg, hgrad,
    kacc, vacc, upd, got, tots, gsum, gtot, inc_out, inc,
    bupd, bgot, bsum, out_out, outg, dwl, dwb, dwp, dwo, dwin,
    l_s, g_s, g_r, t_s, t_r, r1_s, r1_r, r2_s, r2_r, r2t_s, r2t_r, r3_s, r3_r,
    b1_s, b1_r, b2_s, b2_r, b3_s, b3_r, p_s, p_r, w_s, w_r,
):
    tokens = q_ref.shape[0]
    half, quarter = tokens // 2, tokens // 4
    s = lax.axis_index("seq")
    h = lax.axis_index("head")
    g, j = s // INNER, s % INNER
    z, core = s // 2, s % 2
    y, x = h // RING, h % RING

    def head_at(dy, dx):
        return ((y + dy + RING) % RING) * RING + (x + dx + RING) % RING

    inner_peers = [(j + k) % INNER for k in range(1, INNER)]

    gsum[...] = jnp.zeros_like(gsum)
    bsum[...] = jnp.zeros_like(bsum)

    barrier = pltpu.get_barrier_semaphore()

    def greet(seq, head):
        pl.semaphore_signal(barrier, inc=1, device_id=(seq, head), device_id_type=MESH)

    for dy, dx in ((0, 1), (0, -1), (1, 0), (-1, 0)):
        greet(s, head_at(dy, dx))
    greet(2 * z + 1 - core, h)
    for k in range(1, CHIPS):
        greet(2 * ((z + k) % CHIPS) + core, h)
    for k in range(1, RING):
        greet(g * INNER + (j - core + 2 * k) % INNER + 1 - core, h)
    greeted = 4 + 1 + CHIPS - 1 + RING - 1

    loads = [
        pltpu.make_async_copy(src, dst, l_s.at[n])
        for n, (src, dst) in enumerate(
            ((ld_hbm, ld_ref), (k_hbm, k_ref), (v_hbm, v_ref), (q_hbm, q_ref), (og_hbm, full.at[h]), (ow_hbm, ow_ref))
        )
    ]
    for copy in loads:
        copy.start()

    lane = lax.broadcasted_iota(jnp.int32, (DH, DH), 1)
    row = lax.broadcasted_iota(jnp.int32, (DH, DH), 0)
    lower = lane <= row
    offset = jnp.zeros((1, 1), F32)
    loads[0].wait()
    for n in range(tokens // DH):
        piece = jnp.broadcast_to(ld_ref[:, n * DH : (n + 1) * DH], (DH, DH))
        col = jnp.sum(jnp.where(lower, piece, 0.0), axis=1, keepdims=True) + offset
        offset = col[DH - 1 : DH, :]
        wide = jnp.broadcast_to(col, (DH, DH))
        run_col[n * DH : (n + 1) * DH, :] = wide
        run_row[:, n * DH : (n + 1) * DH] = wide.T[0:8, :]
    total = jnp.broadcast_to(offset, (1, DH))
    tots[j] = total

    rc = run_col[...]
    tail = jnp.exp(total - rc)
    loads[1].wait()
    loads[2].wait()
    kt = (k_ref[...].astype(F32) * tail).astype(BF16)
    ktail[...] = kt
    upd[...] = dot(kt, v_ref[...], 0, 0).astype(BF16).reshape(INNER, PIECE, DH)
    got[j] = upd[j]
    vtail[...] = (v_ref[...].astype(F32) * tail).astype(BF16)
    loads[3].wait()
    qgrow[...] = (q_ref[...].astype(F32) * jnp.exp(rc)).astype(BF16)
    loads[4].wait()
    loads[5].wait()

    pl.semaphore_wait(barrier, greeted)

    started = []

    def remote(src, dst, send_sem, recv_sem, seq, head):
        return pltpu.make_async_remote_copy(
            src_ref=src, dst_ref=dst, send_sem=send_sem, recv_sem=recv_sem,
            device_id=(seq, head), device_id_type=MESH,
        )

    def begin(copy, when=None):
        if when is None:
            copy.start()
        else:
            pl.when(when)(copy.start)
        started.append((copy, when))

    def land(copies):
        for copy, when in copies:
            if when is None:
                copy.wait_recv()
            else:
                pl.when(when)(copy.wait_recv)

    def to_inner(src, dst, send_sem, recv_sem):
        out = []
        for k in range(1, INNER):
            p = inner_peers[k - 1]
            piece = dst.at[j] if src is None else src.at[p]
            copy = remote(piece, dst.at[j], send_sem.at[k], recv_sem.at[k], g * INNER + p, h)
            begin(copy)
            out.append((copy, None))
        return out

    def to_outer(dst, send_sem, recv_sem, sign=0):
        out = []
        for k in range(1, GROUPS):
            p = (g + k) % GROUPS if sign == 0 else g + sign * k
            there = (p + GROUPS) % GROUPS
            copy = remote(dst.at[g], dst.at[g], send_sem.at[k], recv_sem.at[k], there * INNER + j, h)
            if sign == 0:
                begin(copy)
                out.append((copy, None))
            else:
                begin(copy, jnp.logical_and(p >= 0, p < GROUPS))
                q = g - sign * k
                out.append((copy, jnp.logical_and(q >= 0, q < GROUPS)))
        return out

    gather = {}
    base = {"A": 0, "B": half}

    def step(kind, first, second):
        return (second, first) if kind == "A" else (first, second)

    def send(name, block, first, count, dy, dx):
        n = len(gather)
        part = full.at[block, pl.ds(first, count)]
        gather[name] = remote(part, part, g_s.at[n], g_r.at[n], s, head_at(dy, dx))
        begin(gather[name])

    def block_of(kind, first, second):
        return head_at(*step(kind, first, second))

    def along(kind, axis, sign):
        return step(kind, sign, 0) if axis == 0 else step(kind, 0, sign)

    def own(kind, axis):
        for sign in (1, -1):
            send((kind, axis, 0, sign), h, base[kind], half, *along(kind, axis, sign))

    def arrived(*name):
        gather[name].wait_recv()

    def relay(kind, axis, off):
        for sign in (1, -1):
            arrived(kind, axis, off, sign)
        for sign in (1, -1):
            block = block_of(kind, -sign, 0) if axis == 0 else block_of(kind, off, -sign)
            part = base[kind] + (0 if sign == 1 else quarter)
            send((kind, axis, off, sign, "far"), block, part, quarter, *along(kind, axis, sign))

    def turn(kind, off):
        for sign in (1, -1):
            send((kind, 1, off, sign), block_of(kind, off, 0), base[kind], half, *along(kind, 1, sign))

    def far(kind, axis, off):
        for sign in (1, -1):
            arrived(kind, axis, off, sign, "far")

    own("A", 0)
    own("B", 0)
    totals_in = to_inner(None, tots, t_s, t_r)
    round1 = to_inner(upd, got, r1_s, r1_r)
    own("B", 1)
    own("A", 1)

    trow = lax.broadcasted_iota(jnp.int32, (TILE, TILE), 0)
    tcol = lax.broadcasted_iota(jnp.int32, (TILE, TILE), 1)
    causal = trow >= tcol
    for t in range(tokens // TILE):
        here = slice(t * TILE, (t + 1) * TILE)
        q = q_ref[here, :]
        here_run = run_col[here, 0:1]
        for u in range(t + 1):
            there = slice(u * TILE, (u + 1) * TILE)
            spread = here_run - run_row[0:1, there]
            if u == t:
                fade = jnp.where(causal, jnp.exp(jnp.where(causal, spread, 0.0)), 0.0)
            else:
                fade = jnp.exp(spread)
            decay[here, there] = fade
            score = dot(q, k_ref[there, :], 1, 1)
            weights[here, there] = (score * fade).astype(BF16)
        n = (t + 1) * TILE
        mixed[here, :] = dot(weights[here, :n], v_ref[:n, :])

    land(totals_in)
    tot = [tots[n] for n in range(INNER)]
    grow = [jnp.exp(t) for t in tot]
    lead = [jnp.zeros((1, DH), F32)]
    for n in range(INNER):
        lead.append(lead[-1] + tot[n])
    gtot[g] = lead[-1]
    round2t = to_outer(gtot, r2t_s, r2t_r)
    land(round1)
    state = jnp.zeros((PIECE, DH), F32)
    before = []
    for n in range(INNER):
        before.append(state)
        state = grow[n] * state + got[n].astype(F32)
    gsum[g] = state
    round2 = to_outer(gsum, r2_s, r2_r, 1)

    relay("A", 0, 0)
    relay("B", 0, 0)
    for off in (-1, 1):
        turn("A", off)
        turn("B", off)
    relay("A", 1, 0)
    relay("B", 1, 0)
    far("A", 0, 0)
    turn("A", 2)
    far("B", 0, 0)
    turn("B", 2)

    def head_part(off, first):
        top, low = slice(0, half), slice(half, tokens)
        b = ((y + off + RING) % RING) * RING
        blocks = jnp.concatenate([full[b + n, top, :] for n in range(RING)], axis=1)
        part_a = dot(blocks, ow_ref[pl.ds(pl.multiple_of(b * DH, DH), RING * DH), :])
        b = (x + off + RING) % RING
        blocks = jnp.concatenate([full[b + RING * n, low, :] for n in range(RING)], axis=1)
        rows = [ow_ref[pl.ds(pl.multiple_of((b + RING * n) * DH, DH), DH), :] for n in range(RING)]
        part_b = dot(blocks, jnp.concatenate(rows, axis=0))
        if first:
            hgrad[top, :] = part_a
            hgrad[low, :] = part_b
        else:
            hgrad[top, :] = hgrad[top, :] + part_a
            hgrad[low, :] = hgrad[low, :] + part_b

    head_part(0, True)

    land(round2t)
    land(round2)
    carried = jnp.zeros((PIECE, DH), F32)
    for n in range(GROUPS):
        carried = jnp.where(n < g, jnp.exp(gtot[n]) * carried + gsum[n], carried)
    for n in range(INNER):
        inc_out[n] = (jnp.exp(lead[n]) * carried + before[n]).astype(BF16)
    inc[j] = inc_out[j]
    round3 = to_inner(inc_out, inc, r3_s, r3_r)

    for off in (-1, 1):
        relay("A", 1, off)
        relay("B", 1, off)

    land(round3)
    incoming = inc[...].reshape(DH, DH)
    whole = mixed[...] + dot(qgrow[...], incoming)
    inv = lax.rsqrt(jnp.mean(whole * whole, axis=1, keepdims=True) + 1e-05)
    normed = whole * inv
    att = normed.astype(BF16)
    att_ref[...] = att
    mixed[...] = normed
    scale[...] = jnp.broadcast_to(inv, (tokens, DH))
    att_t = att.T

    relay("A", 1, 2)
    relay("B", 1, 2)

    near = (0, -1, 1)
    order = [(a, b) for a in near for b in near]
    order += [(0, 2), (2, 0), (-1, 2), (2, -1), (1, 2), (2, 1), (2, 2)]
    blocks = [head_at(a, b) for a, b in order]
    pair_in = []
    owners = []

    def contribute(batch):
        lo, hi = BATCHES[batch]
        for n in range(lo, hi):
            rows = dot(att_t, full[blocks[n]]).T
            dwl[0, n] = rows[: DH // 2, :]
            dwl[1, n] = rows[DH // 2 :, :]
            dwb[n] = dwl[1 - core, n].astype(BF16)
        part = pl.ds(lo, hi - lo)
        copy = remote(dwb.at[part], dwp.at[part], p_s.at[batch], p_r.at[batch], 2 * z + 1 - core, h)
        begin(copy)
        pair_in.append(copy)

    def deliver(batch):
        pair_in[batch].wait_recv()
        for n in range(*BATCHES[batch]):
            dwo[n] = (dwl[core, n] + dwp[n].astype(F32)).astype(BF16)
            f = blocks[n]
            copy = remote(dwo.at[n], dwin.at[z], w_s.at[n], w_r.at[z], 2 * f + core, h)
            begin(copy, f != z)

            @pl.when(f == z)
            def _():
                dwin[z] = dwo[n]

    contribute(0)
    contribute(1)
    contribute(2)
    head_part(-1, False)
    deliver(0)
    deliver(1)
    head_part(1, False)
    deliver(2)

    for off in (0, -1, 1, 2):
        far("A", 1, off)
        far("B", 1, off)

    head_part(2, False)
    normed = mixed[...]
    head_grad = hgrad[...]
    grad = (head_grad - normed * jnp.mean(head_grad * normed, axis=1, keepdims=True)) * scale[...]
    mgrad = grad.astype(BF16)
    mg[...] = mgrad
    bupd[...] = dot(qgrow[...], mgrad, 0, 0).astype(BF16).reshape(INNER, PIECE, DH)
    bgot[j] = bupd[j]
    back1 = to_inner(bupd, bgot, b1_s, b1_r)

    att_t = att_ref[...].T
    contribute(3)
    contribute(4)
    deliver(3)
    deliver(4)

    land(back1)
    state = jnp.zeros((PIECE, DH), F32)
    after = [None] * INNER
    for n in reversed(range(INNER)):
        after[n] = state
        state = bgot[n].astype(F32) + grow[n] * state
    bsum[g] = state
    back2 = to_outer(bsum, b2_s, b2_r, -1)

    for t in range(tokens // TILE):
        here = slice(t * TILE, (t + 1) * TILE)
        n = (t + 1) * TILE
        pair = dot(mg[here, :], v_ref[:n, :], 1, 1)
        masked[here, :n] = (pair * decay[here, :n]).astype(BF16)
        inside = dot(masked[here, :n], k_ref[:n, :])
        grown = (mg[here, :].astype(F32) * jnp.exp(run_col[here, :])).astype(BF16)
        qg_ref[here, :] = (inside + dot(grown, incoming, 1, 1)).astype(BF16)
    for u in range(tokens // TILE):
        there = slice(u * TILE, (u + 1) * TILE)
        m = u * TILE
        kacc[there, :] = dot(masked[m:, there], q_ref[m:, :], 0, 0)
        vacc[there, :] = dot(weights[m:, there], mg[m:, :], 0, 0)

    land(back2)
    trail = [None] * INNER
    ahead = jnp.zeros((1, DH), F32)
    for n in reversed(range(INNER)):
        trail[n] = ahead
        ahead = ahead + tot[n]
    carried = jnp.zeros((PIECE, DH), F32)
    for n in reversed(range(GROUPS)):
        carried = jnp.where(n > g, bsum[n] + jnp.exp(gtot[n]) * carried, carried)
    for n in range(INNER):
        out_out[n] = (after[n] + jnp.exp(trail[n]) * carried).astype(BF16)
    outg[j] = out_out[j]
    back3 = to_inner(out_out, outg, b3_s, b3_r)

    land(back3)
    outgoing = outg[...].reshape(DH, DH)
    kg_ref[...] = (kacc[...] + dot(vtail[...], outgoing, 1, 1)).astype(BF16)
    vg_ref[...] = (vacc[...] + dot(ktail[...], outgoing)).astype(BF16)

    for n in range(CHIPS):
        copy = remote(dwo.at[0], dwin.at[n], w_s.at[0], w_r.at[n], s, h)
        pl.when(n != z)(copy.wait_recv)
    acc = dwin[0].astype(F32)
    for n in range(1, CHIPS):
        acc = acc + dwin[n].astype(F32)
    wg_ref[...] = acc.astype(BF16)

    for copy, when in started:
        if when is None:
            copy.wait_send()
        else:
            pl.when(when)(copy.wait_send)


def hand_out(*refs):
    n = len(refs) // 2
    sem = refs[-1]
    copies = [pltpu.make_async_copy(refs[i], refs[n + i], sem.at[i]) for i in range(n)]
    for copy in copies:
        copy.start()
    for copy in copies:
        copy.wait()


def on_device(queries, keys, values, log_decay, out_weight, out_grad):
    tokens = queries.shape[0]
    vmem = pl.BlockSpec(memory_space=pltpu.VMEM)
    anywhere = pl.BlockSpec(memory_space=pl.ANY)
    rows = out_weight.shape[0] // (GROUPS * INNER)
    shapes = ((tokens, DH),) * 4 + ((rows, DH),)
    dma = pltpu.SemaphoreType.DMA
    inner, outer = dma((INNER,)), dma((GROUPS,))
    blocks = RING * RING
    scratch = [
        *[pltpu.VMEM((tokens, DH), BF16)] * 3,
        pltpu.VMEM((1, tokens), F32),
        pltpu.VMEM(out_weight.shape, BF16),
        pltpu.VMEM((blocks, tokens, DH), BF16),
        pltpu.VMEM((tokens, DH), F32),
        pltpu.VMEM((8, tokens), F32),
        *[pltpu.VMEM((tokens, DH), BF16)] * 3,
        pltpu.VMEM((tokens, tokens), BF16),
        pltpu.VMEM((tokens, tokens), F32),
        pltpu.VMEM((tokens, tokens), BF16),
        *[pltpu.VMEM((tokens, DH), F32)] * 2,
        pltpu.VMEM((tokens, DH), BF16),
        *[pltpu.VMEM((tokens, DH), F32)] * 3,
        *[pltpu.VMEM((INNER, PIECE, DH), BF16)] * 2,
        pltpu.VMEM((INNER, 1, DH), F32),
        pltpu.VMEM((GROUPS, PIECE, DH), F32),
        pltpu.VMEM((GROUPS, 1, DH), F32),
        *[pltpu.VMEM((INNER, PIECE, DH), BF16)] * 4,
        pltpu.VMEM((GROUPS, PIECE, DH), F32),
        *[pltpu.VMEM((INNER, PIECE, DH), BF16)] * 2,
        pltpu.VMEM((2, blocks, rows, DH), F32),
        *[pltpu.VMEM((blocks, rows, DH), BF16)] * 4,
        dma((6,)),
        dma((40,)), dma((40,)),
        inner, inner,
        inner, inner, outer, outer, outer, outer, inner, inner,
        inner, inner, outer, outer, inner, inner,
        dma((len(BATCHES),)), dma((len(BATCHES),)), dma((blocks,)), dma((CHIPS,)),
    ]
    results = pl.pallas_call(
        kernel,
        out_shape=tuple(pltpu.VMEM(shape, BF16) for shape in shapes),
        in_specs=[anywhere] * 6,
        out_specs=(vmem,) * 5,
        scratch_shapes=scratch,
        compiler_params=pltpu.CompilerParams(collective_id=0, has_side_effects=True),
    )(queries, keys, values, log_decay, out_weight, out_grad)
    return pl.pallas_call(
        hand_out,
        out_shape=tuple(jax.ShapeDtypeStruct(shape, BF16) for shape in shapes),
        in_specs=[vmem] * 5,
        out_specs=(anywhere,) * 5,
        scratch_shapes=[dma((5,))],
    )(*[pltpu.with_memory_space_constraint(array, pltpu.VMEM) for array in results])


def solution(mesh):
    return jax.shard_map(
        on_device,
        mesh=mesh,
        in_specs=(
            P("seq", "head"),
            P("seq", "head"),
            P("seq", "head"),
            P("head", "seq"),
            P(None, "head"),
            P("seq", "head"),
        ),
        out_specs=(P("seq", "head"),) * 5,
        check_vma=False,
    )
```

```python
import jax
import jax.numpy as jnp
from jax import lax
from jax.experimental import pallas as pl
from jax.experimental.pallas import tpu as pltpu
from jax.sharding import PartitionSpec as P

MESH = pl.DeviceIdType.MESH
F32 = jnp.float32
BF16 = jnp.bfloat16
GROUPS = 4
INNER = 8
CHIPS = 16
RING = 4
TILE = 256
DH = 128
PIECE = DH // INNER
BATCHES = ((0, 4), (4, 8), (8, 11), (11, 16))


def dot(a, b, ca=1, cb=0):
    return lax.dot_general(a, b, (((ca,), (cb,)), ((), ())), preferred_element_type=F32)


def kernel(
    q_hbm, k_hbm, v_hbm, ld_hbm, ow_hbm, og_hbm,
    att_ref, qg_ref, kg_ref, vg_ref, wg_ref,
    q_ref, k_ref, v_ref, ld_ref, ow_ref,
    full, run_col, run_row, qgrow, ktail, vtail, weights, decay, masked, mixed, scale, mg, hgrad,
    kacc, vacc, upd, got, tots, gsum, gtot, inc_out, inc,
    bupd, bgot, bsum, out_out, outg, dwl, dwb, dwp, dwo, dwq, dws, dwin,
    l_s, g_s, g_r, t_s, t_r, r1_s, r1_r, r2_s, r2_r, r2t_s, r2t_r, r3_s, r3_r,
    b1_s, b1_r, b2_s, b2_r, b3_s, b3_r, p_s, p_r, q_s, q_r, w_s, w_r, heard,
):
    tokens = q_ref.shape[0]
    half, quarter = tokens // 2, tokens // 4
    s = lax.axis_index("seq")
    h = lax.axis_index("head")
    g, j = s // INNER, s % INNER
    z, core = s // 2, s % 2
    y, x = h // RING, h % RING

    def head_at(dy, dx):
        return ((y + dy + RING) % RING) * RING + (x + dx + RING) % RING

    inner_peers = [(j + k) % INNER for k in range(1, INNER)]

    gsum[...] = jnp.zeros_like(gsum)
    bsum[...] = jnp.zeros_like(bsum)

    barrier = pltpu.get_barrier_semaphore()
    for seq, head in (
        (s, head_at(0, 1)), (s, head_at(0, -1)), (s, head_at(1, 0)), (s, head_at(-1, 0)), (2 * z + 1 - core, h),
        (2 * ((z + 1) % CHIPS) + core, h), (2 * ((z + CHIPS - 1) % CHIPS) + core, h),
    ):
        pl.semaphore_signal(barrier, inc=1, device_id=(seq, head), device_id_type=MESH)

    def tell(n):
        for sign in (1, -1):
            there = 2 * ((z + CHIPS + sign * 2**n) % CHIPS) + core
            pl.semaphore_signal(heard.at[n], inc=1, device_id=(there, h), device_id_type=MESH)

    def hear(n):
        pl.semaphore_wait(heard.at[n], 2)

    loads = [
        pltpu.make_async_copy(src, dst, l_s.at[n])
        for n, (src, dst) in enumerate(
            ((ld_hbm, ld_ref), (k_hbm, k_ref), (v_hbm, v_ref), (q_hbm, q_ref), (og_hbm, full.at[h]), (ow_hbm, ow_ref))
        )
    ]
    for copy in loads:
        copy.start()

    lane = lax.broadcasted_iota(jnp.int32, (DH, DH), 1)
    row = lax.broadcasted_iota(jnp.int32, (DH, DH), 0)
    lower = lane <= row
    offset = jnp.zeros((1, 1), F32)
    loads[0].wait()
    for n in range(tokens // DH):
        piece = jnp.broadcast_to(ld_ref[:, n * DH : (n + 1) * DH], (DH, DH))
        col = jnp.sum(jnp.where(lower, piece, 0.0), axis=1, keepdims=True) + offset
        offset = col[DH - 1 : DH, :]
        wide = jnp.broadcast_to(col, (DH, DH))
        run_col[n * DH : (n + 1) * DH, :] = wide
        run_row[:, n * DH : (n + 1) * DH] = wide.T[0:8, :]
    total = jnp.broadcast_to(offset, (1, DH))
    tots[j] = total

    rc = run_col[...]
    tail = jnp.exp(total - rc)
    loads[1].wait()
    loads[2].wait()
    kt = (k_ref[...].astype(F32) * tail).astype(BF16)
    ktail[...] = kt
    upd[...] = dot(kt, v_ref[...], 0, 0).astype(BF16).reshape(INNER, PIECE, DH)
    got[j] = upd[j]
    vtail[...] = (v_ref[...].astype(F32) * tail).astype(BF16)
    loads[3].wait()
    qgrow[...] = (q_ref[...].astype(F32) * jnp.exp(rc)).astype(BF16)
    loads[4].wait()
    loads[5].wait()

    pl.semaphore_wait(barrier, 7)
    tell(0)

    started = []

    def remote(src, dst, send_sem, recv_sem, seq, head):
        return pltpu.make_async_remote_copy(
            src_ref=src, dst_ref=dst, send_sem=send_sem, recv_sem=recv_sem,
            device_id=(seq, head), device_id_type=MESH,
        )

    def begin(copy, when=None):
        if when is None:
            copy.start()
        else:
            pl.when(when)(copy.start)
            started.append((copy, when))

    def bytes_of(ref, send_sem, recv_sem):
        return remote(ref, ref, send_sem, recv_sem, s, h)

    def land(copies):
        for copy, when in copies:
            if when is None:
                copy.wait_recv()
            else:
                pl.when(when)(copy.wait_recv)

    def to_inner(src, dst, send_sem, recv_sem):
        for p in inner_peers:
            piece = dst.at[j] if src is None else src.at[p]
            begin(remote(piece, dst.at[j], send_sem, recv_sem, g * INNER + p, h))
        every = bytes_of(dst.at[pl.ds(0, INNER - 1)], send_sem, recv_sem)
        started.append((every, None))
        return [(every, None)]

    def to_outer(dst, send_sem, recv_sem, sign=0):
        out = []
        for k in range(1, GROUPS):
            p = (g + k) % GROUPS if sign == 0 else g + sign * k
            there = (p + GROUPS) % GROUPS
            copy = remote(dst.at[g], dst.at[g], send_sem.at[k - 1], recv_sem.at[k - 1], there * INNER + j, h)
            if sign == 0:
                begin(copy)
                started.append((copy, None))
                out.append((copy, None))
            else:
                begin(copy, jnp.logical_and(p >= 0, p < GROUPS))
                q = g - sign * k
                out.append((copy, jnp.logical_and(q >= 0, q < GROUPS)))
        return out

    gather = {}
    base = {"A": 0, "B": half}

    def step(kind, first, second):
        return (second, first) if kind == "A" else (first, second)

    def send(name, block, first, count, dy, dx):
        n = len(gather)
        part = full.at[block, pl.ds(first, count)]
        gather[name] = remote(part, part, g_s, g_r.at[n], s, head_at(dy, dx))
        begin(gather[name])

    def block_of(kind, first, second):
        return head_at(*step(kind, first, second))

    def along(kind, axis, sign):
        return step(kind, sign, 0) if axis == 0 else step(kind, 0, sign)

    def own(kind, axis):
        for sign in (1, -1):
            send((kind, axis, 0, sign), h, base[kind], half, *along(kind, axis, sign))

    def arrived(*name):
        gather[name].wait_recv()

    def relay(kind, axis, off):
        for sign in (1, -1):
            arrived(kind, axis, off, sign)
        for sign in (1, -1):
            block = block_of(kind, -sign, 0) if axis == 0 else block_of(kind, off, -sign)
            part = base[kind] + (0 if sign == 1 else quarter)
            send((kind, axis, off, sign, "far"), block, part, quarter, *along(kind, axis, sign))

    def turn(kind, off):
        for sign in (1, -1):
            send((kind, 1, off, sign), block_of(kind, off, 0), base[kind], half, *along(kind, 1, sign))

    def far(kind, axis, off):
        for sign in (1, -1):
            arrived(kind, axis, off, sign, "far")

    own("A", 0)
    own("B", 0)
    own("B", 1)
    own("A", 1)

    trow = lax.broadcasted_iota(jnp.int32, (TILE, TILE), 0)
    tcol = lax.broadcasted_iota(jnp.int32, (TILE, TILE), 1)
    causal = trow >= tcol
    def local(t):
        here = slice(t * TILE, (t + 1) * TILE)
        q = q_ref[here, :]
        here_run = run_col[here, 0:1]
        for u in range(t + 1):
            there = slice(u * TILE, (u + 1) * TILE)
            spread = here_run - run_row[0:1, there]
            if u == t:
                fade = jnp.where(causal, jnp.exp(jnp.where(causal, spread, 0.0)), 0.0)
            else:
                fade = jnp.exp(spread)
            decay[here, there] = fade
            score = dot(q, k_ref[there, :], 1, 1)
            weights[here, there] = (score * fade).astype(BF16)
        n = (t + 1) * TILE
        mixed[here, :] = dot(weights[here, :n], v_ref[:n, :])

    local(0)
    hear(0)
    tell(1)
    local(1)
    local(2)
    hear(1)
    tell(2)
    totals_in = to_inner(None, tots, t_s, t_r)
    round1 = to_inner(upd, got, r1_s, r1_r)
    local(3)

    relay("A", 0, 0)
    relay("B", 0, 0)
    for off in (-1, 1):
        turn("A", off)
        turn("B", off)

    land(totals_in)
    tot = [tots[n] for n in range(INNER)]
    grow = [jnp.exp(t) for t in tot]
    lead = [jnp.zeros((1, DH), F32)]
    for n in range(INNER):
        lead.append(lead[-1] + tot[n])
    gtot[g] = lead[-1]
    hear(2)
    round2t = to_outer(gtot, r2t_s, r2t_r)
    land(round1)
    state = jnp.zeros((PIECE, DH), F32)
    before = []
    for n in range(INNER):
        before.append(state)
        state = grow[n] * state + got[n].astype(F32)
    gsum[g] = state
    round2 = to_outer(gsum, r2_s, r2_r, 1)

    relay("A", 1, 0)
    relay("B", 1, 0)
    far("A", 0, 0)
    turn("A", 2)
    far("B", 0, 0)
    turn("B", 2)

    def head_part(off, first):
        top, low = slice(0, half), slice(half, tokens)
        b = ((y + off + RING) % RING) * RING
        blocks = jnp.concatenate([full[b + n, top, :] for n in range(RING)], axis=1)
        part_a = dot(blocks, ow_ref[pl.ds(pl.multiple_of(b * DH, DH), RING * DH), :])
        b = (x + off + RING) % RING
        blocks = jnp.concatenate([full[b + RING * n, low, :] for n in range(RING)], axis=1)
        rows = [ow_ref[pl.ds(pl.multiple_of((b + RING * n) * DH, DH), DH), :] for n in range(RING)]
        part_b = dot(blocks, jnp.concatenate(rows, axis=0))
        if first:
            hgrad[top, :] = part_a
            hgrad[low, :] = part_b
        else:
            hgrad[top, :] = hgrad[top, :] + part_a
            hgrad[low, :] = hgrad[low, :] + part_b

    head_part(0, True)

    land(round2t)
    land(round2)
    carried = jnp.zeros((PIECE, DH), F32)
    for n in range(GROUPS):
        carried = jnp.where(n < g, jnp.exp(gtot[n]) * carried + gsum[n], carried)
    for n in range(INNER):
        inc_out[n] = (jnp.exp(lead[n]) * carried + before[n]).astype(BF16)
    inc[j] = inc_out[j]
    round3 = to_inner(inc_out, inc, r3_s, r3_r)

    for off in (-1, 1):
        relay("A", 1, off)
        relay("B", 1, off)

    land(round3)
    incoming = inc[...].reshape(DH, DH)
    whole = mixed[...] + dot(qgrow[...], incoming)
    inv = lax.rsqrt(jnp.mean(whole * whole, axis=1, keepdims=True) + 1e-05)
    normed = whole * inv
    att = normed.astype(BF16)
    att_ref[...] = att
    mixed[...] = normed
    scale[...] = jnp.broadcast_to(inv, (tokens, DH))
    att_t = att.T

    near = (0, -1, 1)
    order = [(a, b) for a in near for b in near]
    order += [(0, 2), (2, 0), (-1, 2), (2, -1), (1, 2), (2, 1), (2, 2)]
    blocks = [head_at(a, b) for a, b in order]
    pair_in = []
    other = z + 1 - 2 * (z % 2)

    def contribute(batch):
        lo, hi = BATCHES[batch]
        for n in range(lo, hi):
            rows = dot(att_t, full[blocks[n]]).T
            dwl[0, n] = rows[: DH // 2, :]
            dwl[1, n] = rows[DH // 2 :, :]
            dwb[n] = dwl[1 - core, n].astype(BF16)
        part = pl.ds(lo, hi - lo)
        copy = remote(dwb.at[part], dwp.at[part], p_s.at[batch], p_r.at[batch], 2 * z + 1 - core, h)
        begin(copy)
        started.append((copy, None))
        pair_in.append(copy)

    def ours(n):
        return blocks[n] % 2 == z % 2

    def across(n):
        return remote(dwo.at[n], dwq.at[n], q_s, q_r.at[n], 2 * other + core, h)

    def pair_up(batch):
        pair_in[batch].wait_recv()
        for n in range(*BATCHES[batch]):
            both = dwl[core, n] + dwp[n].astype(F32)
            dwl[core, n] = both
            dwo[n] = both.astype(BF16)
            pl.when(jnp.logical_not(ours(n)))(across(n).start)

    def deliver(batch):
        for n in range(*BATCHES[batch]):
            f = blocks[n]

            @pl.when(ours(n))
            def _():
                across(n).wait_recv()
                dws[n] = (dwl[core, n] + dwq[n].astype(F32)).astype(BF16)
                copy = remote(dws.at[n], dwin.at[z // 2], w_s, w_r, 2 * f + core, h)
                pl.when(f != z)(copy.start)

                @pl.when(f == z)
                def _():
                    dwin[z // 2] = dws[n]

    contribute(0)
    contribute(1)
    pair_up(0)
    far("A", 1, 0)
    far("B", 1, 0)
    contribute(2)
    pair_up(1)
    pair_up(2)
    relay("A", 1, 2)
    relay("B", 1, 2)
    head_part(-1, False)
    head_part(1, False)
    deliver(0)
    deliver(1)

    for off in (-1, 1, 2):
        far("A", 1, off)
        far("B", 1, off)

    head_part(2, False)
    normed = mixed[...]
    head_grad = hgrad[...]
    grad = (head_grad - normed * jnp.mean(head_grad * normed, axis=1, keepdims=True)) * scale[...]
    mgrad = grad.astype(BF16)
    mg[...] = mgrad
    bupd[...] = dot(qgrow[...], mgrad, 0, 0).astype(BF16).reshape(INNER, PIECE, DH)
    bgot[j] = bupd[j]
    back1 = to_inner(bupd, bgot, b1_s, b1_r)

    att_t = att_ref[...].T
    contribute(3)
    deliver(2)

    for t in range(tokens // TILE):
        here = slice(t * TILE, (t + 1) * TILE)
        n = (t + 1) * TILE
        pair = dot(mg[here, :], v_ref[:n, :], 1, 1)
        masked[here, :n] = (pair * decay[here, :n]).astype(BF16)
        inside = dot(masked[here, :n], k_ref[:n, :])
        grown = (mg[here, :].astype(F32) * jnp.exp(run_col[here, :])).astype(BF16)
        qg_ref[here, :] = (inside + dot(grown, incoming, 1, 1)).astype(BF16)

    pair_up(3)

    land(back1)
    state = jnp.zeros((PIECE, DH), F32)
    after = [None] * INNER
    for n in reversed(range(INNER)):
        after[n] = state
        state = bgot[n].astype(F32) + grow[n] * state
    bsum[g] = state
    back2 = to_outer(bsum, b2_s, b2_r, -1)

    deliver(3)
    for u in range(tokens // TILE):
        there = slice(u * TILE, (u + 1) * TILE)
        m = u * TILE
        kacc[there, :] = dot(masked[m:, there], q_ref[m:, :], 0, 0)
        vacc[there, :] = dot(weights[m:, there], mg[m:, :], 0, 0)

    land(back2)
    trail = [None] * INNER
    ahead = jnp.zeros((1, DH), F32)
    for n in reversed(range(INNER)):
        trail[n] = ahead
        ahead = ahead + tot[n]
    carried = jnp.zeros((PIECE, DH), F32)
    for n in reversed(range(GROUPS)):
        carried = jnp.where(n > g, bsum[n] + jnp.exp(gtot[n]) * carried, carried)
    for n in range(INNER):
        out_out[n] = (after[n] + jnp.exp(trail[n]) * carried).astype(BF16)
    outg[j] = out_out[j]
    back3 = to_inner(out_out, outg, b3_s, b3_r)

    land(back3)
    outgoing = outg[...].reshape(DH, DH)
    kg_ref[...] = (kacc[...] + dot(vtail[...], outgoing, 1, 1)).astype(BF16)
    vg_ref[...] = (vacc[...] + dot(ktail[...], outgoing)).astype(BF16)

    weights_in = bytes_of(dwin.at[pl.ds(0, CHIPS // 2 - 1)], w_s, w_r)
    weights_in.wait_recv()
    acc = dwin[0].astype(F32)
    for n in range(1, CHIPS // 2):
        acc = acc + dwin[n].astype(F32)
    wg_ref[...] = acc.astype(BF16)

    weights_in.wait_send()
    bytes_of(dwo.at[pl.ds(0, CHIPS // 2)], q_s, q_r.at[0]).wait_send()
    bytes_of(full.at[pl.ds(0, RING * RING - 1)], g_s, g_r.at[0]).wait_send()
    for copy, when in started:
        if when is None:
            copy.wait_send()
        else:
            pl.when(when)(copy.wait_send)


def hand_out(*refs):
    n = len(refs) // 2
    sem = refs[-1]
    copies = [pltpu.make_async_copy(refs[i], refs[n + i], sem.at[i]) for i in range(n)]
    for copy in copies:
        copy.start()
    for copy in copies:
        copy.wait()


def on_device(queries, keys, values, log_decay, out_weight, out_grad):
    tokens = queries.shape[0]
    vmem = pl.BlockSpec(memory_space=pltpu.VMEM)
    anywhere = pl.BlockSpec(memory_space=pl.ANY)
    rows = out_weight.shape[0] // (GROUPS * INNER)
    shapes = ((tokens, DH),) * 4 + ((rows, DH),)
    dma = pltpu.SemaphoreType.DMA
    inner, outer = dma, dma((GROUPS - 1,))
    blocks = RING * RING
    scratch = [
        *[pltpu.VMEM((tokens, DH), BF16)] * 3,
        pltpu.VMEM((1, tokens), F32),
        pltpu.VMEM(out_weight.shape, BF16),
        pltpu.VMEM((blocks, tokens, DH), BF16),
        pltpu.VMEM((tokens, DH), F32),
        pltpu.VMEM((8, tokens), F32),
        *[pltpu.VMEM((tokens, DH), BF16)] * 3,
        pltpu.VMEM((tokens, tokens), BF16),
        pltpu.VMEM((tokens, tokens), F32),
        pltpu.VMEM((tokens, tokens), BF16),
        *[pltpu.VMEM((tokens, DH), F32)] * 2,
        pltpu.VMEM((tokens, DH), BF16),
        *[pltpu.VMEM((tokens, DH), F32)] * 3,
        *[pltpu.VMEM((INNER, PIECE, DH), BF16)] * 2,
        pltpu.VMEM((INNER, 1, DH), F32),
        pltpu.VMEM((GROUPS, PIECE, DH), F32),
        pltpu.VMEM((GROUPS, 1, DH), F32),
        *[pltpu.VMEM((INNER, PIECE, DH), BF16)] * 4,
        pltpu.VMEM((GROUPS, PIECE, DH), F32),
        *[pltpu.VMEM((INNER, PIECE, DH), BF16)] * 2,
        pltpu.VMEM((2, blocks, rows, DH), F32),
        *[pltpu.VMEM((blocks, rows, DH), BF16)] * 5,
        pltpu.VMEM((CHIPS // 2, rows, DH), BF16),
        dma((6,)),
        dma, dma((40,)),
        inner, inner,
        inner, inner, outer, outer, outer, outer, inner, inner,
        inner, inner, outer, outer, inner, inner,
        dma((len(BATCHES),)), dma((len(BATCHES),)), dma, dma((blocks,)), dma, dma,
        pltpu.SemaphoreType.REGULAR((3,)),
    ]
    results = pl.pallas_call(
        kernel,
        out_shape=tuple(pltpu.VMEM(shape, BF16) for shape in shapes),
        in_specs=[anywhere] * 6,
        out_specs=(vmem,) * 5,
        scratch_shapes=scratch,
        compiler_params=pltpu.CompilerParams(collective_id=0, has_side_effects=True),
    )(queries, keys, values, log_decay, out_weight, out_grad)
    return pl.pallas_call(
        hand_out,
        out_shape=tuple(jax.ShapeDtypeStruct(shape, BF16) for shape in shapes),
        in_specs=[vmem] * 5,
        out_specs=(anywhere,) * 5,
        scratch_shapes=[dma((5,))],
    )(*[pltpu.with_memory_space_constraint(array, pltpu.VMEM) for array in results])


def solution(mesh):
    return jax.shard_map(
        on_device,
        mesh=mesh,
        in_specs=(
            P("seq", "head"),
            P("seq", "head"),
            P("seq", "head"),
            P("head", "seq"),
            P(None, "head"),
            P("seq", "head"),
        ),
        out_specs=(P("seq", "head"),) * 5,
        check_vma=False,
    )
```

```python
import jax
import jax.numpy as jnp
from jax import lax
from jax.experimental import pallas as pl
from jax.experimental.pallas import tpu as pltpu
from jax.sharding import PartitionSpec as P

MESH = pl.DeviceIdType.MESH
F32 = jnp.float32
BF16 = jnp.bfloat16
GROUPS = 4
INNER = 8
CHIPS = 16
RING = 4
TILE = 256
DH = 128
PIECE = DH // INNER
BATCHES = ((0, 4), (4, 8), (8, 11), (11, 16))


def dot(a, b, ca=1, cb=0):
    return lax.dot_general(a, b, (((ca,), (cb,)), ((), ())), preferred_element_type=F32)


def kernel(
    q_hbm, k_hbm, v_hbm, ld_hbm, ow_hbm, og_hbm,
    att_ref, qg_ref, kg_ref, vg_ref, wg_ref,
    q_ref, k_ref, v_ref, ld_ref, ow_ref,
    full, run_col, run_row, qgrow, ktail, vtail, weights, decay, masked, mixed, scale, mg, hgrad,
    kacc, vacc, upd, got, tots, gsum, gtot, inc_out, inc,
    bupd, bgot, bsum, bown, swap, out_out, outg, dwl, dwb, dwp, dwo, dwq, dws, dwin,
    l_s, g_s, g_r, t_s, t_r, r1_s, r1_r, r2_s, r2_r, r2t_s, r2t_r, r3_s, r3_r,
    b1_s, b1_r, b2_s, b2_r, b3_s, b3_r, s_s, s_r, p_s, p_r, q_s, q_r, w_s, w_r, heard,
):
    tokens = q_ref.shape[0]
    half, quarter = tokens // 2, tokens // 4
    s = lax.axis_index("seq")
    h = lax.axis_index("head")
    g, j = s // INNER, s % INNER
    z, core = s // 2, s % 2
    y, x = h // RING, h % RING

    def head_at(dy, dx):
        return ((y + dy + RING) % RING) * RING + (x + dx + RING) % RING

    inner_peers = [(j + k) % INNER for k in range(1, INNER)]

    gsum[...] = jnp.zeros_like(gsum)
    bsum[...] = jnp.zeros_like(bsum)

    barrier = pltpu.get_barrier_semaphore()
    for seq, head in (
        (s, head_at(0, 1)), (s, head_at(0, -1)), (s, head_at(1, 0)), (s, head_at(-1, 0)), (2 * z + 1 - core, h),
        (2 * ((z + 1) % CHIPS) + core, h), (2 * ((z + CHIPS - 1) % CHIPS) + core, h),
    ):
        pl.semaphore_signal(barrier, inc=1, device_id=(seq, head), device_id_type=MESH)

    def tell(n):
        for sign in (1, -1):
            there = 2 * ((z + CHIPS + sign * 2**n) % CHIPS) + core
            pl.semaphore_signal(heard.at[n], inc=1, device_id=(there, h), device_id_type=MESH)

    def hear(n):
        pl.semaphore_wait(heard.at[n], 2)

    loads = [
        pltpu.make_async_copy(src, dst, l_s.at[n])
        for n, (src, dst) in enumerate(
            ((ld_hbm, ld_ref), (k_hbm, k_ref), (v_hbm, v_ref), (q_hbm, q_ref), (og_hbm, full.at[h]), (ow_hbm, ow_ref))
        )
    ]
    for copy in loads:
        copy.start()

    pl.semaphore_wait(barrier, 7)
    tell(0)

    started = []

    def remote(src, dst, send_sem, recv_sem, seq, head):
        return pltpu.make_async_remote_copy(
            src_ref=src, dst_ref=dst, send_sem=send_sem, recv_sem=recv_sem,
            device_id=(seq, head), device_id_type=MESH,
        )

    def begin(copy, when=None):
        if when is None:
            copy.start()
        else:
            pl.when(when)(copy.start)
            started.append((copy, when))

    def bytes_of(ref, send_sem, recv_sem):
        return remote(ref, ref, send_sem, recv_sem, s, h)

    def land(copies):
        for copy, when in copies:
            if when is None:
                copy.wait_recv()
            else:
                pl.when(when)(copy.wait_recv)

    def to_inner(src, dst, send_sem, recv_sem):
        for p in inner_peers:
            piece = dst.at[j] if src is None else src.at[p]
            begin(remote(piece, dst.at[j], send_sem, recv_sem, g * INNER + p, h))
        every = bytes_of(dst.at[pl.ds(0, INNER - 1)], send_sem, recv_sem)
        started.append((every, None))
        return [(every, None)]

    def to_outer(dst, send_sem, recv_sem, sign=0):
        out = []
        for k in range(1, GROUPS):
            p = (g + k) % GROUPS if sign == 0 else g + sign * k
            there = (p + GROUPS) % GROUPS
            copy = remote(dst.at[g], dst.at[g], send_sem.at[k - 1], recv_sem.at[k - 1], there * INNER + j, h)
            if sign == 0:
                begin(copy)
                started.append((copy, None))
                out.append((copy, None))
            else:
                begin(copy, jnp.logical_and(p >= 0, p < GROUPS))
                q = g - sign * k
                out.append((copy, jnp.logical_and(q >= 0, q < GROUPS)))
        return out

    gather = {}
    base = {"A": 0, "B": half}

    def step(kind, first, second):
        return (second, first) if kind == "A" else (first, second)

    def send(group, block, first, count, dy, dx, src=None):
        n = gather.setdefault(group, len(gather))
        part = full.at[block, pl.ds(first, count)]
        begin(remote(part if src is None else src.at[pl.ds(first, count)], part, g_s, g_r.at[n], s, head_at(dy, dx)))

    def arrived(group, blocks):
        rows = blocks if blocks is not None else full.at[0, pl.ds(0, half)]
        bytes_of(rows, g_s, g_r.at[gather[group]]).wait_recv()

    def far_group(kind, axis, off):
        if axis == 0:
            return ("first", kind)
        return ("middle",) if off == 0 else ("last",)

    def block_of(kind, first, second):
        return head_at(*step(kind, first, second))

    def along(kind, axis, sign):
        return step(kind, sign, 0) if axis == 0 else step(kind, 0, sign)

    def own(kind, axis):
        for sign in (1, -1):
            send((kind, axis, 0), h, base[kind], half, *along(kind, axis, sign), src=og_hbm)

    def relay(kind, axis, off):
        arrived((kind, axis, off), full.at[0])
        for sign in (1, -1):
            block = block_of(kind, -sign, 0) if axis == 0 else block_of(kind, off, -sign)
            part = base[kind] + (0 if sign == 1 else quarter)
            send(far_group(kind, axis, off), block, part, quarter, *along(kind, axis, sign))

    def turn(kind, off):
        for sign in (1, -1):
            send((kind, 1, off), block_of(kind, off, 0), base[kind], half, *along(kind, 1, sign))

    own("A", 0)
    own("B", 0)
    own("B", 1)
    own("A", 1)

    lane = lax.broadcasted_iota(jnp.int32, (DH, DH), 1)
    row = lax.broadcasted_iota(jnp.int32, (DH, DH), 0)
    lower = lane <= row
    offset = jnp.zeros((1, 1), F32)
    loads[0].wait()
    for n in range(tokens // DH):
        piece = jnp.broadcast_to(ld_ref[:, n * DH : (n + 1) * DH], (DH, DH))
        col = jnp.sum(jnp.where(lower, piece, 0.0), axis=1, keepdims=True) + offset
        offset = col[DH - 1 : DH, :]
        wide = jnp.broadcast_to(col, (DH, DH))
        run_col[n * DH : (n + 1) * DH, :] = wide
        run_row[:, n * DH : (n + 1) * DH] = wide.T[0:8, :]
    total = jnp.broadcast_to(offset, (1, DH))
    tots[j] = total

    hear(0)
    tell(1)

    rc = run_col[...]
    tail = jnp.exp(total - rc)
    loads[1].wait()
    loads[2].wait()
    kt = (k_ref[...].astype(F32) * tail).astype(BF16)
    ktail[...] = kt
    upd[...] = dot(kt, v_ref[...], 0, 0).astype(BF16).reshape(INNER, PIECE, DH)
    got[j] = upd[j]
    vtail[...] = (v_ref[...].astype(F32) * tail).astype(BF16)
    loads[3].wait()
    qgrow[...] = (q_ref[...].astype(F32) * jnp.exp(rc)).astype(BF16)
    loads[4].wait()
    loads[5].wait()

    trow = lax.broadcasted_iota(jnp.int32, (TILE, TILE), 0)
    tcol = lax.broadcasted_iota(jnp.int32, (TILE, TILE), 1)
    causal = trow >= tcol
    def local(t):
        here = slice(t * TILE, (t + 1) * TILE)
        q = q_ref[here, :]
        here_run = run_col[here, 0:1]
        for u in range(t + 1):
            there = slice(u * TILE, (u + 1) * TILE)
            spread = here_run - run_row[0:1, there]
            if u == t:
                fade = jnp.where(causal, jnp.exp(jnp.where(causal, spread, 0.0)), 0.0)
            else:
                fade = jnp.exp(spread)
            decay[here, there] = fade
            score = dot(q, k_ref[there, :], 1, 1)
            weights[here, there] = (score * fade).astype(BF16)
        n = (t + 1) * TILE
        mixed[here, :] = dot(weights[here, :n], v_ref[:n, :])

    local(0)
    local(1)
    hear(1)
    tell(2)
    totals_in = to_inner(None, tots, t_s, t_r)
    round1 = to_inner(upd, got, r1_s, r1_r)
    local(2)
    local(3)

    relay("A", 0, 0)
    relay("B", 0, 0)
    for off in (-1, 1):
        turn("A", off)
        turn("B", off)

    land(totals_in)
    tot = [tots[n] for n in range(INNER)]
    grow = [jnp.exp(t) for t in tot]
    lead = [jnp.zeros((1, DH), F32)]
    for n in range(INNER):
        lead.append(lead[-1] + tot[n])
    gtot[g] = lead[-1]
    hear(2)
    round2t = to_outer(gtot, r2t_s, r2t_r)
    land(round1)
    state = jnp.zeros((PIECE, DH), F32)
    before = []
    for n in range(INNER):
        before.append(state)
        state = grow[n] * state + got[n].astype(F32)
    gsum[g] = state
    round2 = to_outer(gsum, r2_s, r2_r, 1)

    relay("A", 1, 0)
    relay("B", 1, 0)
    arrived(("first", "A"), None)
    turn("A", 2)
    arrived(("first", "B"), None)
    turn("B", 2)

    def head_part(off, first):
        top, low = slice(0, half), slice(half, tokens)
        b = ((y + off + RING) % RING) * RING
        blocks = jnp.concatenate([full[b + n, top, :] for n in range(RING)], axis=1)
        part_a = dot(blocks, ow_ref[pl.ds(pl.multiple_of(b * DH, DH), RING * DH), :])
        b = (x + off + RING) % RING
        blocks = jnp.concatenate([full[b + RING * n, low, :] for n in range(RING)], axis=1)
        rows = [ow_ref[pl.ds(pl.multiple_of((b + RING * n) * DH, DH), DH), :] for n in range(RING)]
        part_b = dot(blocks, jnp.concatenate(rows, axis=0))
        if first:
            hgrad[top, :] = part_a
            hgrad[low, :] = part_b
        else:
            hgrad[top, :] = hgrad[top, :] + part_a
            hgrad[low, :] = hgrad[low, :] + part_b

    head_part(0, True)

    land(round2t)
    land(round2)
    carried = jnp.zeros((PIECE, DH), F32)
    for n in range(GROUPS):
        carried = jnp.where(n < g, jnp.exp(gtot[n]) * carried + gsum[n], carried)
    for n in range(INNER):
        inc_out[n] = (jnp.exp(lead[n]) * carried + before[n]).astype(BF16)
    inc[j] = inc_out[j]
    round3 = to_inner(inc_out, inc, r3_s, r3_r)

    for off in (-1, 1):
        relay("A", 1, off)
        relay("B", 1, off)

    land(round3)
    incoming = inc[...].reshape(DH, DH)
    whole = mixed[...] + dot(qgrow[...], incoming)
    inv = lax.rsqrt(jnp.mean(whole * whole, axis=1, keepdims=True) + 1e-05)
    normed = whole * inv
    att = normed.astype(BF16)
    att_ref[...] = att
    mixed[...] = normed
    scale[...] = jnp.broadcast_to(inv, (tokens, DH))
    att_t = att.T

    near = (0, -1, 1)
    order = [(a, b) for a in near for b in near]
    order += [(0, 2), (2, 0), (-1, 2), (2, -1), (1, 2), (2, 1), (2, 2)]
    blocks = [head_at(a, b) for a, b in order]
    pair_in = []
    other = z + 1 - 2 * (z % 2)

    def contribute(batch):
        lo, hi = BATCHES[batch]
        for n in range(lo, hi):
            rows = dot(att_t, full[blocks[n]]).T
            dwl[0, n] = rows[: DH // 2, :]
            dwl[1, n] = rows[DH // 2 :, :]
            dwb[n] = dwl[1 - core, n].astype(BF16)
        part = pl.ds(lo, hi - lo)
        copy = remote(dwb.at[part], dwp.at[part], p_s.at[batch], p_r.at[batch], 2 * z + 1 - core, h)
        begin(copy)
        started.append((copy, None))
        pair_in.append(copy)

    def ours(n):
        return blocks[n] % 2 == z % 2

    def across(n):
        return remote(dwo.at[n], dwq.at[n], q_s, q_r.at[n], 2 * other + core, h)

    def pair_up(batch):
        pair_in[batch].wait_recv()
        for n in range(*BATCHES[batch]):
            both = dwl[core, n] + dwp[n].astype(F32)
            dwl[core, n] = both
            dwo[n] = both.astype(BF16)
            pl.when(jnp.logical_not(ours(n)))(across(n).start)

    def deliver(batch):
        for n in range(*BATCHES[batch]):
            f = blocks[n]

            @pl.when(ours(n))
            def _():
                across(n).wait_recv()
                dws[n] = (dwl[core, n] + dwq[n].astype(F32)).astype(BF16)
                copy = remote(dws.at[n], dwin.at[z // 2], w_s, w_r, 2 * f + core, h)
                pl.when(f != z)(copy.start)

                @pl.when(f == z)
                def _():
                    dwin[z // 2] = dws[n]

    contribute(0)
    contribute(1)
    pair_up(0)
    arrived(("middle",), full.at[0])
    contribute(2)
    pair_up(1)
    pair_up(2)
    relay("A", 1, 2)
    relay("B", 1, 2)
    head_part(-1, False)
    head_part(1, False)
    deliver(0)
    deliver(1)

    arrived(("last",), full.at[pl.ds(0, 3)])

    head_part(2, False)
    normed = mixed[...]
    head_grad = hgrad[...]
    grad = (head_grad - normed * jnp.mean(head_grad * normed, axis=1, keepdims=True)) * scale[...]
    mgrad = grad.astype(BF16)
    mg[...] = mgrad
    bupd[...] = dot(qgrow[...], mgrad, 0, 0).astype(BF16).reshape(INNER, PIECE, DH)
    bgot[j] = bupd[j]
    back1 = to_inner(bupd, bgot, b1_s, b1_r)

    att_t = att_ref[...].T
    contribute(3)
    deliver(2)

    for t in range(tokens // TILE):
        here = slice(t * TILE, (t + 1) * TILE)
        n = (t + 1) * TILE
        pair = dot(mg[here, :], v_ref[:n, :], 1, 1)
        masked[here, :n] = (pair * decay[here, :n]).astype(BF16)
        inside = dot(masked[here, :n], k_ref[:n, :])
        grown = (mg[here, :].astype(F32) * jnp.exp(run_col[here, :])).astype(BF16)
        qg_ref[here, :] = (inside + dot(grown, incoming, 1, 1)).astype(BF16)

    pair_up(3)

    land(back1)
    state = jnp.zeros((PIECE, DH), F32)
    after = [None] * INNER
    for n in reversed(range(INNER)):
        after[n] = state
        state = bgot[n].astype(F32) + grow[n] * state
    bown[...] = state.astype(BF16)
    back2 = []
    for k in (2, 1, 3):
        p = g - k
        for m in range(RING):
            there = (p + GROUPS) % GROUPS * INNER + (j + 2 * m) % INNER
            copy = remote(bown, bsum.at[g, j // 2], b2_s.at[k - 1], b2_r.at[k - 1], there, h)
            pl.when(p >= 0)(copy.start)
        every = bytes_of(bsum.at[0], b2_s.at[k - 1], b2_r.at[k - 1])
        started.append((every, p >= 0))
        back2.append((every, g + k < GROUPS))
    for n in range(INNER):
        out_out[n] = after[n].astype(BF16)
    outg[j] = out_out[j]
    back3 = to_inner(out_out, outg, b3_s, b3_r)

    deliver(3)
    for u in range(tokens // TILE):
        there = slice(u * TILE, (u + 1) * TILE)
        m = u * TILE
        kacc[there, :] = dot(masked[m:, there], q_ref[m:, :], 0, 0)
        vacc[there, :] = dot(weights[m:, there], mg[m:, :], 0, 0)

    land(back2)
    trail = jnp.zeros((1, DH), F32)
    for n in range(INNER):
        trail = trail + jnp.where(n > j, tot[n], 0.0)
    carried = jnp.zeros((RING, PIECE, DH), F32)
    for n in reversed(range(GROUPS)):
        carried = jnp.where(n > g, bsum[n].astype(F32) + jnp.exp(gtot[n])[None] * carried, carried)
    swap[core] = carried
    copy = remote(swap.at[core], swap.at[core], s_s, s_r, 2 * z + 1 - core, h)
    begin(copy)
    started.append((copy, None))
    land(back3)
    copy.wait_recv()
    rows = jnp.concatenate([swap[n % 2, n // 2] for n in range(INNER)], axis=0)
    outgoing = (outg[...].reshape(DH, DH).astype(F32) + jnp.exp(trail) * rows).astype(BF16)
    kg_ref[...] = (kacc[...] + dot(vtail[...], outgoing, 1, 1)).astype(BF16)
    vg_ref[...] = (vacc[...] + dot(ktail[...], outgoing)).astype(BF16)

    weights_in = bytes_of(dwin.at[pl.ds(0, CHIPS // 2 - 1)], w_s, w_r)
    weights_in.wait_recv()
    acc = dwin[0].astype(F32)
    for n in range(1, CHIPS // 2):
        acc = acc + dwin[n].astype(F32)
    wg_ref[...] = acc.astype(BF16)

    weights_in.wait_send()
    bytes_of(dwo.at[pl.ds(0, CHIPS // 2)], q_s, q_r.at[0]).wait_send()
    bytes_of(full.at[pl.ds(0, RING * RING - 1)], g_s, g_r.at[0]).wait_send()
    for copy, when in started:
        if when is None:
            copy.wait_send()
        else:
            pl.when(when)(copy.wait_send)


def hand_out(*refs):
    n = len(refs) // 2
    sem = refs[-1]
    copies = [pltpu.make_async_copy(refs[i], refs[n + i], sem.at[i]) for i in range(n)]
    for copy in copies:
        copy.start()
    for copy in copies:
        copy.wait()


def on_device(queries, keys, values, log_decay, out_weight, out_grad):
    tokens = queries.shape[0]
    vmem = pl.BlockSpec(memory_space=pltpu.VMEM)
    anywhere = pl.BlockSpec(memory_space=pl.ANY)
    rows = out_weight.shape[0] // (GROUPS * INNER)
    shapes = ((tokens, DH),) * 4 + ((rows, DH),)
    dma = pltpu.SemaphoreType.DMA
    inner, outer = dma, dma((GROUPS - 1,))
    blocks = RING * RING
    scratch = [
        *[pltpu.VMEM((tokens, DH), BF16)] * 3,
        pltpu.VMEM((1, tokens), F32),
        pltpu.VMEM(out_weight.shape, BF16),
        pltpu.VMEM((blocks, tokens, DH), BF16),
        pltpu.VMEM((tokens, DH), F32),
        pltpu.VMEM((8, tokens), F32),
        *[pltpu.VMEM((tokens, DH), BF16)] * 3,
        pltpu.VMEM((tokens, tokens), BF16),
        pltpu.VMEM((tokens, tokens), F32),
        pltpu.VMEM((tokens, tokens), BF16),
        *[pltpu.VMEM((tokens, DH), F32)] * 2,
        pltpu.VMEM((tokens, DH), BF16),
        *[pltpu.VMEM((tokens, DH), F32)] * 3,
        *[pltpu.VMEM((INNER, PIECE, DH), BF16)] * 2,
        pltpu.VMEM((INNER, 1, DH), F32),
        pltpu.VMEM((GROUPS, PIECE, DH), F32),
        pltpu.VMEM((GROUPS, 1, DH), F32),
        *[pltpu.VMEM((INNER, PIECE, DH), BF16)] * 4,
        pltpu.VMEM((GROUPS, RING, PIECE, DH), BF16),
        pltpu.VMEM((PIECE, DH), BF16),
        pltpu.VMEM((2, RING, PIECE, DH), F32),
        *[pltpu.VMEM((INNER, PIECE, DH), BF16)] * 2,
        pltpu.VMEM((2, blocks, rows, DH), F32),
        *[pltpu.VMEM((blocks, rows, DH), BF16)] * 5,
        pltpu.VMEM((CHIPS // 2, rows, DH), BF16),
        dma((6,)),
        dma, dma((14,)),
        inner, inner,
        inner, inner, outer, outer, outer, outer, inner, inner,
        inner, inner, outer, outer, inner, inner, dma, dma,
        dma((len(BATCHES),)), dma((len(BATCHES),)), dma, dma((blocks,)), dma, dma,
        pltpu.SemaphoreType.REGULAR((3,)),
    ]
    results = pl.pallas_call(
        kernel,
        out_shape=tuple(pltpu.VMEM(shape, BF16) for shape in shapes),
        in_specs=[anywhere] * 6,
        out_specs=(vmem,) * 5,
        scratch_shapes=scratch,
        compiler_params=pltpu.CompilerParams(collective_id=0, has_side_effects=True),
    )(queries, keys, values, log_decay, out_weight, out_grad)
    return pl.pallas_call(
        hand_out,
        out_shape=tuple(jax.ShapeDtypeStruct(shape, BF16) for shape in shapes),
        in_specs=[vmem] * 5,
        out_specs=(anywhere,) * 5,
        scratch_shapes=[dma((5,))],
    )(*[pltpu.with_memory_space_constraint(array, pltpu.VMEM) for array in results])


def solution(mesh):
    return jax.shard_map(
        on_device,
        mesh=mesh,
        in_specs=(
            P("seq", "head"),
            P("seq", "head"),
            P("seq", "head"),
            P("head", "seq"),
            P(None, "head"),
            P("seq", "head"),
        ),
        out_specs=(P("seq", "head"),) * 5,
        check_vma=False,
    )
```

```python
import jax
import jax.numpy as jnp
from jax import lax
from jax.experimental import pallas as pl
from jax.experimental.pallas import tpu as pltpu
from jax.sharding import PartitionSpec as P

MESH = pl.DeviceIdType.MESH
F32 = jnp.float32
BF16 = jnp.bfloat16
GROUPS = 4
INNER = 8
CHIPS = 16
RING = 4
TILE = 256
DH = 128
PIECE = DH // INNER
BATCHES = ((0, 4), (4, 8), (8, 11), (11, 16))


def dot(a, b, ca=1, cb=0):
    return lax.dot_general(a, b, (((ca,), (cb,)), ((), ())), preferred_element_type=F32)


def kernel(
    q_hbm, k_hbm, v_hbm, ld_hbm, ow_hbm, og_hbm,
    att_ref, qg_ref, kg_ref, vg_ref, wg_ref,
    q_ref, k_ref, v_ref, ld_ref, ow_ref,
    full, run_col, run_row, qgrow, qgt, ktail, vtail, weights, decay, masked, mixed, scale, mg, hgrad,
    kacc, vacc, upd, got, tots, gsum, gown, fswap, gtot, inc_out, inc,
    bupd, bgot, bsum, bown, swap, out_out, outg, dwl, dwb, dwp, dwo, dwq, dws, dwin,
    l_s, g_s, g_r, t_s, t_r, r1_s, r1_r, r2_s, r2_r, r2t_s, r2t_r, r3_s, r3_r, f_s, f_r,
    b1_s, b1_r, b2_s, b2_r, b3_s, b3_r, s_s, s_r, p_s, p_r, q_s, q_r, w_s, w_r, heard,
):
    tokens = q_ref.shape[0]
    half, quarter = tokens // 2, tokens // 4
    s = lax.axis_index("seq")
    h = lax.axis_index("head")
    g, j = s // INNER, s % INNER
    z, core = s // 2, s % 2
    y, x = h // RING, h % RING

    def head_at(dy, dx):
        return ((y + dy + RING) % RING) * RING + (x + dx + RING) % RING

    inner_peers = [(j + k) % INNER for k in range(1, INNER)]

    gsum[...] = jnp.zeros_like(gsum)
    bsum[...] = jnp.zeros_like(bsum)

    barrier = pltpu.get_barrier_semaphore()
    for seq, head in (
        (s, head_at(0, 1)), (s, head_at(0, -1)), (s, head_at(1, 0)), (s, head_at(-1, 0)), (2 * z + 1 - core, h),
        (2 * ((z + 1) % CHIPS) + core, h), (2 * ((z + CHIPS - 1) % CHIPS) + core, h),
    ):
        pl.semaphore_signal(barrier, inc=1, device_id=(seq, head), device_id_type=MESH)

    def tell(n):
        for sign in (1, -1):
            there = 2 * ((z + CHIPS + sign * 2**n) % CHIPS) + core
            pl.semaphore_signal(heard.at[n], inc=1, device_id=(there, h), device_id_type=MESH)

    def hear(n):
        pl.semaphore_wait(heard.at[n], 2)

    loads = [
        pltpu.make_async_copy(src, dst, l_s.at[n])
        for n, (src, dst) in enumerate(
            ((ld_hbm, ld_ref), (k_hbm, k_ref), (v_hbm, v_ref), (q_hbm, q_ref), (og_hbm, full.at[h]), (ow_hbm, ow_ref))
        )
    ]
    for copy in loads:
        copy.start()

    pl.semaphore_wait(barrier, 7)
    tell(0)

    started = []

    def remote(src, dst, send_sem, recv_sem, seq, head):
        return pltpu.make_async_remote_copy(
            src_ref=src, dst_ref=dst, send_sem=send_sem, recv_sem=recv_sem,
            device_id=(seq, head), device_id_type=MESH,
        )

    def begin(copy, when=None):
        if when is None:
            copy.start()
        else:
            pl.when(when)(copy.start)
            started.append((copy, when))

    def bytes_of(ref, send_sem, recv_sem):
        return remote(ref, ref, send_sem, recv_sem, s, h)

    def spread(src, dst, send_sem, recv_sem, sign):
        out = []
        for k in (2, 1, 3):
            p = g + sign * k
            inside = jnp.logical_and(p >= 0, p < GROUPS)
            for m in range(RING):
                there = (p + GROUPS) % GROUPS * INNER + (j + 2 * m) % INNER
                copy = remote(src, dst.at[g, j // 2], send_sem.at[k - 1], recv_sem.at[k - 1], there, h)
                pl.when(inside)(copy.start)
            every = bytes_of(dst.at[0], send_sem.at[k - 1], recv_sem.at[k - 1])
            started.append((every, inside))
            out.append((every, jnp.logical_and(g - sign * k >= 0, g - sign * k < GROUPS)))
        return out

    def exchange(buffer, send_sem, recv_sem):
        copy = remote(buffer.at[core], buffer.at[core], send_sem, recv_sem, 2 * z + 1 - core, h)
        begin(copy)
        started.append((copy, None))
        return copy

    def stacked(buffer):
        return jnp.concatenate([buffer[n % 2, n // 2] for n in range(INNER)], axis=0)

    def land(copies):
        for copy, when in copies:
            if when is None:
                copy.wait_recv()
            else:
                pl.when(when)(copy.wait_recv)

    def drain(copies):
        for copy, when in copies:
            if when is None:
                copy.wait_send()
            else:
                pl.when(when)(copy.wait_send)

    def to_inner(src, dst, send_sem, recv_sem):
        for p in inner_peers:
            piece = dst.at[j] if src is None else src.at[p]
            begin(remote(piece, dst.at[j], send_sem, recv_sem, g * INNER + p, h))
        every = bytes_of(dst.at[pl.ds(0, INNER - 1)], send_sem, recv_sem)
        started.append((every, None))
        return [(every, None)]

    def to_outer(dst, send_sem, recv_sem):
        for k in range(1, GROUPS):
            begin(remote(dst.at[g], dst.at[g], send_sem, recv_sem, (g + k) % GROUPS * INNER + j, h))
        every = bytes_of(dst.at[pl.ds(0, GROUPS - 1)], send_sem, recv_sem)
        started.append((every, None))
        return [(every, None)]

    gather = {}
    base = {"A": 0, "B": half}

    def step(kind, first, second):
        return (second, first) if kind == "A" else (first, second)

    def send(group, block, first, count, dy, dx, src=None):
        n = gather.setdefault(group, len(gather))
        part = full.at[block, pl.ds(first, count)]
        begin(remote(part if src is None else src.at[pl.ds(first, count)], part, g_s, g_r.at[n], s, head_at(dy, dx)))

    def arrived(group, blocks):
        rows = blocks if blocks is not None else full.at[0, pl.ds(0, half)]
        bytes_of(rows, g_s, g_r.at[gather[group]]).wait_recv()

    def far_group(kind, axis, off):
        if axis == 0:
            return ("first", kind)
        return ("middle",) if off == 0 else ("last", abs(off))

    def block_of(kind, first, second):
        return head_at(*step(kind, first, second))

    def along(kind, axis, sign):
        return step(kind, sign, 0) if axis == 0 else step(kind, 0, sign)

    def quarters(kind, axis, off, sign, block, src=None):
        part, late = (0, quarter) if sign == 1 else (quarter, 0)
        way = along(kind, axis, sign)
        send((kind, axis, off), block, base[kind] + part, quarter, *way, src=src)
        if axis == 0:
            group = ("rest", 0)
        else:
            group = ("rest", 1) if off != 2 else ("rest", 2)
        send(group, block, base[kind] + late, quarter, *way, src=src)

    def own(kind, axis):
        for sign in (1, -1):
            quarters(kind, axis, 0, sign, h, og_hbm)

    def relay(kind, axis, off):
        arrived((kind, axis, off), None)
        for sign in (1, -1):
            block = block_of(kind, -sign, 0) if axis == 0 else block_of(kind, off, -sign)
            part = base[kind] + (0 if sign == 1 else quarter)
            send(far_group(kind, axis, off), block, part, quarter, *along(kind, axis, sign))

    def turn(kind, off):
        for sign in (1, -1):
            quarters(kind, 1, off, sign, block_of(kind, off, 0))

    own("A", 0)
    own("B", 0)
    own("B", 1)
    own("A", 1)

    lane = lax.broadcasted_iota(jnp.int32, (DH, DH), 1)
    row = lax.broadcasted_iota(jnp.int32, (DH, DH), 0)
    lower = lane <= row
    offset = jnp.zeros((1, 1), F32)
    loads[0].wait()
    for n in range(tokens // DH):
        piece = jnp.broadcast_to(ld_ref[:, n * DH : (n + 1) * DH], (DH, DH))
        col = jnp.sum(jnp.where(lower, piece, 0.0), axis=1, keepdims=True) + offset
        offset = col[DH - 1 : DH, :]
        wide = jnp.broadcast_to(col, (DH, DH))
        run_col[n * DH : (n + 1) * DH, :] = wide
        run_row[:, n * DH : (n + 1) * DH] = wide.T[0:8, :]
    total = jnp.broadcast_to(offset, (1, DH))
    tots[j] = total

    hear(0)
    tell(1)

    rc = run_col[...]
    tail = jnp.exp(total - rc)
    loads[1].wait()
    loads[2].wait()
    kt = (k_ref[...].astype(F32) * tail).astype(BF16)
    ktail[...] = kt
    upd[...] = dot(kt, v_ref[...], 0, 0).astype(BF16).reshape(INNER, PIECE, DH)
    got[j] = upd[j]
    vtail[...] = (v_ref[...].astype(F32) * tail).astype(BF16)
    loads[3].wait()
    qgrow[...] = (q_ref[...].astype(F32) * jnp.exp(rc)).astype(BF16)
    loads[4].wait()
    loads[5].wait()

    trow = lax.broadcasted_iota(jnp.int32, (TILE, TILE), 0)
    tcol = lax.broadcasted_iota(jnp.int32, (TILE, TILE), 1)
    causal = trow >= tcol
    def local(t):
        here = slice(t * TILE, (t + 1) * TILE)
        q = q_ref[here, :]
        here_run = run_col[here, 0:1]
        for u in range(t + 1):
            there = slice(u * TILE, (u + 1) * TILE)
            spread = here_run - run_row[0:1, there]
            if u == t:
                fade = jnp.where(causal, jnp.exp(jnp.where(causal, spread, 0.0)), 0.0)
            else:
                fade = jnp.exp(spread)
            decay[here, there] = fade
            score = dot(q, k_ref[there, :], 1, 1)
            weights[here, there] = (score * fade).astype(BF16)
        n = (t + 1) * TILE
        mixed[here, :] = dot(weights[here, :n], v_ref[:n, :])

    local(0)
    local(1)
    hear(1)
    tell(2)
    totals_in = to_inner(None, tots, t_s, t_r)
    round1 = to_inner(upd, got, r1_s, r1_r)
    local(2)
    local(3)

    relay("A", 0, 0)
    relay("B", 0, 0)
    arrived(("rest", 0), full.at[0])
    for off in (-1, 1):
        turn("A", off)
        turn("B", off)

    land(totals_in)
    tot = [tots[n] for n in range(INNER)]
    grow = [jnp.exp(t) for t in tot]
    everything = tot[0]
    for n in range(1, INNER):
        everything = everything + tot[n]
    gtot[g] = everything
    hear(2)
    round2t = to_outer(gtot, r2t_s, r2t_r)
    land(round1)
    state = jnp.zeros((PIECE, DH), F32)
    before = []
    for n in range(INNER):
        before.append(state)
        state = grow[n] * state + got[n].astype(F32)
    gown[...] = state.astype(BF16)
    round2 = spread(gown, gsum, r2_s, r2_r, 1)
    for n in range(INNER):
        inc_out[n] = before[n].astype(BF16)
    inc[j] = inc_out[j]
    round3 = to_inner(inc_out, inc, r3_s, r3_r)

    relay("A", 1, 0)
    relay("B", 1, 0)
    arrived(("first", "A"), None)
    turn("A", 2)
    arrived(("first", "B"), None)
    turn("B", 2)

    def head_part(off, first):
        top, low = slice(0, half), slice(half, tokens)
        b = ((y + off + RING) % RING) * RING
        blocks = jnp.concatenate([full[b + n, top, :] for n in range(RING)], axis=1)
        part_a = dot(blocks, ow_ref[pl.ds(pl.multiple_of(b * DH, DH), RING * DH), :])
        b = (x + off + RING) % RING
        blocks = jnp.concatenate([full[b + RING * n, low, :] for n in range(RING)], axis=1)
        rows = [ow_ref[pl.ds(pl.multiple_of((b + RING * n) * DH, DH), DH), :] for n in range(RING)]
        part_b = dot(blocks, jnp.concatenate(rows, axis=0))
        if first:
            hgrad[top, :] = part_a
            hgrad[low, :] = part_b
        else:
            hgrad[top, :] = hgrad[top, :] + part_a
            hgrad[low, :] = hgrad[low, :] + part_b

    def head_rest(offsets):
        for rows, at in ((slice(0, half), lambda n: head_at(2, n)), (slice(half, tokens), lambda n: head_at(n, 2))):
            blocks = [full[at(n), rows, :] for n in offsets]
            wide = [ow_ref[pl.ds(pl.multiple_of(at(n) * DH, DH), DH), :] for n in offsets]
            if len(offsets) > 1:
                part = dot(jnp.concatenate(blocks, axis=1), jnp.concatenate(wide, axis=0))
            else:
                part = dot(blocks[0], wide[0])
            hgrad[rows, :] = hgrad[rows, :] + part

    head_part(0, True)

    land(round2t)
    land(round2)
    carried = jnp.zeros((RING, PIECE, DH), F32)
    for n in range(GROUPS):
        carried = jnp.where(n < g, jnp.exp(gtot[n])[None] * carried + gsum[n].astype(F32), carried)
    fswap[core] = carried
    swapped = exchange(fswap, f_s, f_r)

    for off in (-1, 1):
        relay("A", 1, off)
        relay("B", 1, off)

    land(round3)
    swapped.wait_recv()
    head = jnp.zeros((1, DH), F32)
    for n in range(INNER):
        head = head + jnp.where(n < j, tot[n], 0.0)
    incoming = (inc[...].reshape(DH, DH).astype(F32) + jnp.exp(head) * stacked(fswap)).astype(BF16)
    whole = mixed[...] + dot(qgrow[...], incoming)
    inv = lax.rsqrt(jnp.mean(whole * whole, axis=1, keepdims=True) + 1e-05)
    normed = whole * inv
    att = normed.astype(BF16)
    att_ref[...] = att
    mixed[...] = normed
    scale[...] = jnp.broadcast_to(inv, (tokens, DH))
    att_t = att.T
    qgt[...] = qgrow[...].T

    near = (0, -1, 1)
    order = [(a, b) for a in near for b in near]
    order += [(0, 2), (2, 0), (-1, 2), (2, -1), (1, 2), (2, 1), (2, 2)]
    blocks = [head_at(a, b) for a, b in order]
    pair_in = []
    other = z + 1 - 2 * (z % 2)

    def contribute(batch):
        lo, hi = BATCHES[batch]
        for n in range(lo, hi):
            rows = dot(att_t, full[blocks[n]]).T
            dwl[0, n] = rows[: DH // 2, :]
            dwl[1, n] = rows[DH // 2 :, :]
            dwb[n] = dwl[1 - core, n].astype(BF16)
        part = pl.ds(lo, hi - lo)
        copy = remote(dwb.at[part], dwp.at[part], p_s.at[batch], p_r.at[batch], 2 * z + 1 - core, h)
        begin(copy)
        started.append((copy, None))
        pair_in.append(copy)

    def ours(n):
        return blocks[n] % 2 == z % 2

    def across(n):
        return remote(dwo.at[n], dwq.at[n], q_s, q_r.at[n], 2 * other + core, h)

    def pair_up(batch):
        pair_in[batch].wait_recv()
        for n in range(*BATCHES[batch]):
            both = dwl[core, n] + dwp[n].astype(F32)
            dwl[core, n] = both
            dwo[n] = both.astype(BF16)
            pl.when(jnp.logical_not(ours(n)))(across(n).start)

    def deliver(batch):
        for n in range(*BATCHES[batch]):
            f = blocks[n]

            @pl.when(ours(n))
            def _():
                across(n).wait_recv()
                dws[n] = (dwl[core, n] + dwq[n].astype(F32)).astype(BF16)
                copy = remote(dws.at[n], dwin.at[z // 2], w_s, w_r, 2 * f + core, h)
                pl.when(f != z)(copy.start)

                @pl.when(f == z)
                def _():
                    dwin[z // 2] = dws[n]

    arrived(("rest", 1), full.at[pl.ds(0, 3)])
    contribute(0)
    contribute(1)
    pair_up(0)
    arrived(("middle",), full.at[0])
    contribute(2)
    pair_up(1)
    relay("A", 1, 2)
    relay("B", 1, 2)
    pair_up(2)
    arrived(("rest", 2), full.at[0])
    head_part(-1, False)
    head_part(1, False)
    deliver(0)
    deliver(1)
    deliver(2)

    arrived(("last", 1), full.at[pl.ds(0, 2)])
    head_rest((0, -1, 1))
    arrived(("last", 2), full.at[0])

    head_rest((2,))
    normed = mixed[...]
    head_grad = hgrad[...]
    grad = (head_grad - normed * jnp.mean(head_grad * normed, axis=1, keepdims=True)) * scale[...]
    mgrad = grad.astype(BF16)
    mg[...] = mgrad
    bupd[...] = dot(qgt[...], mgrad).astype(BF16).reshape(INNER, PIECE, DH)
    bgot[j] = bupd[j]
    back1 = to_inner(bupd, bgot, b1_s, b1_r)

    att_t = att_ref[...].T
    contribute(3)
    for t in range(tokens // TILE):
        here = slice(t * TILE, (t + 1) * TILE)
        n = (t + 1) * TILE
        pair = dot(mg[here, :], v_ref[:n, :], 1, 1)
        masked[here, :n] = (pair * decay[here, :n]).astype(BF16)
        inside = dot(masked[here, :n], k_ref[:n, :])
        grown = (mg[here, :].astype(F32) * jnp.exp(run_col[here, :])).astype(BF16)
        qg_ref[here, :] = (inside + dot(grown, incoming, 1, 1)).astype(BF16)

    pair_up(3)

    land(back1)
    state = jnp.zeros((PIECE, DH), F32)
    after = [None] * INNER
    for n in reversed(range(INNER)):
        after[n] = state
        state = bgot[n].astype(F32) + grow[n] * state
    bown[...] = state.astype(BF16)
    back2 = spread(bown, bsum, b2_s, b2_r, -1)
    for n in range(INNER):
        out_out[n] = after[n].astype(BF16)
    outg[j] = out_out[j]
    back3 = to_inner(out_out, outg, b3_s, b3_r)

    deliver(3)
    for u in range(tokens // TILE):
        there = slice(u * TILE, (u + 1) * TILE)
        m = u * TILE
        kacc[there, :] = dot(masked[m:, there], q_ref[m:, :], 0, 0)
        vacc[there, :] = dot(weights[m:, there], mg[m:, :], 0, 0)

    drain(started[:-4])
    del started[:-4]
    bytes_of(full.at[pl.ds(0, RING * RING - 1)], g_s, g_r.at[0]).wait_send()

    land(back2)
    trail = jnp.zeros((1, DH), F32)
    for n in range(INNER):
        trail = trail + jnp.where(n > j, tot[n], 0.0)
    carried = jnp.zeros((RING, PIECE, DH), F32)
    for n in reversed(range(GROUPS)):
        carried = jnp.where(n > g, bsum[n].astype(F32) + jnp.exp(gtot[n])[None] * carried, carried)
    swap[core] = carried
    swapped = exchange(swap, s_s, s_r)
    land(back3)
    swapped.wait_recv()
    outgoing = (outg[...].reshape(DH, DH).astype(F32) + jnp.exp(trail) * stacked(swap)).astype(BF16)
    kg_ref[...] = (kacc[...] + dot(vtail[...], outgoing, 1, 1)).astype(BF16)
    vg_ref[...] = (vacc[...] + dot(ktail[...], outgoing)).astype(BF16)

    weights_in = bytes_of(dwin.at[pl.ds(0, CHIPS // 2 - 1)], w_s, w_r)
    weights_in.wait_recv()
    acc = dwin[0].astype(F32)
    for n in range(1, CHIPS // 2):
        acc = acc + dwin[n].astype(F32)
    wg_ref[...] = acc.astype(BF16)

    weights_in.wait_send()
    bytes_of(dwo.at[pl.ds(0, CHIPS // 2)], q_s, q_r.at[0]).wait_send()
    drain(started)


def hand_out(*refs):
    n = len(refs) // 2
    sem = refs[-1]
    copies = [pltpu.make_async_copy(refs[i], refs[n + i], sem.at[i]) for i in range(n)]
    for copy in copies:
        copy.start()
    for copy in copies:
        copy.wait()


def on_device(queries, keys, values, log_decay, out_weight, out_grad):
    tokens = queries.shape[0]
    vmem = pl.BlockSpec(memory_space=pltpu.VMEM)
    anywhere = pl.BlockSpec(memory_space=pl.ANY)
    rows = out_weight.shape[0] // (GROUPS * INNER)
    shapes = ((tokens, DH),) * 4 + ((rows, DH),)
    dma = pltpu.SemaphoreType.DMA
    inner, outer = dma, dma((GROUPS - 1,))
    blocks = RING * RING
    scratch = [
        *[pltpu.VMEM((tokens, DH), BF16)] * 3,
        pltpu.VMEM((1, tokens), F32),
        pltpu.VMEM(out_weight.shape, BF16),
        pltpu.VMEM((blocks, tokens, DH), BF16),
        pltpu.VMEM((tokens, DH), F32),
        pltpu.VMEM((8, tokens), F32),
        pltpu.VMEM((tokens, DH), BF16),
        pltpu.VMEM((DH, tokens), BF16),
        *[pltpu.VMEM((tokens, DH), BF16)] * 2,
        pltpu.VMEM((tokens, tokens), BF16),
        pltpu.VMEM((tokens, tokens), F32),
        pltpu.VMEM((tokens, tokens), BF16),
        *[pltpu.VMEM((tokens, DH), F32)] * 2,
        pltpu.VMEM((tokens, DH), BF16),
        *[pltpu.VMEM((tokens, DH), F32)] * 3,
        *[pltpu.VMEM((INNER, PIECE, DH), BF16)] * 2,
        pltpu.VMEM((INNER, 1, DH), F32),
        pltpu.VMEM((GROUPS, RING, PIECE, DH), BF16),
        pltpu.VMEM((PIECE, DH), BF16),
        pltpu.VMEM((2, RING, PIECE, DH), F32),
        pltpu.VMEM((GROUPS, 1, DH), F32),
        *[pltpu.VMEM((INNER, PIECE, DH), BF16)] * 4,
        pltpu.VMEM((GROUPS, RING, PIECE, DH), BF16),
        pltpu.VMEM((PIECE, DH), BF16),
        pltpu.VMEM((2, RING, PIECE, DH), F32),
        *[pltpu.VMEM((INNER, PIECE, DH), BF16)] * 2,
        pltpu.VMEM((2, blocks, rows, DH), F32),
        *[pltpu.VMEM((blocks, rows, DH), BF16)] * 5,
        pltpu.VMEM((CHIPS // 2, rows, DH), BF16),
        dma((6,)),
        dma, dma((18,)),
        inner, inner,
        inner, inner, outer, outer, dma, dma, inner, inner, dma, dma,
        inner, inner, outer, outer, inner, inner, dma, dma,
        dma((len(BATCHES),)), dma((len(BATCHES),)), dma, dma((blocks,)), dma, dma,
        pltpu.SemaphoreType.REGULAR((3,)),
    ]
    results = pl.pallas_call(
        kernel,
        out_shape=tuple(pltpu.VMEM(shape, BF16) for shape in shapes),
        in_specs=[anywhere] * 6,
        out_specs=(vmem,) * 5,
        scratch_shapes=scratch,
        compiler_params=pltpu.CompilerParams(collective_id=0, has_side_effects=True),
    )(queries, keys, values, log_decay, out_weight, out_grad)
    return pl.pallas_call(
        hand_out,
        out_shape=tuple(jax.ShapeDtypeStruct(shape, BF16) for shape in shapes),
        in_specs=[vmem] * 5,
        out_specs=(anywhere,) * 5,
        scratch_shapes=[dma((5,))],
    )(*[pltpu.with_memory_space_constraint(array, pltpu.VMEM) for array in results])


def solution(mesh):
    return jax.shard_map(
        on_device,
        mesh=mesh,
        in_specs=(
            P("seq", "head"),
            P("seq", "head"),
            P("seq", "head"),
            P("head", "seq"),
            P(None, "head"),
            P("seq", "head"),
        ),
        out_specs=(P("seq", "head"),) * 5,
        check_vma=False,
    )
```

```python
import jax
import jax.numpy as jnp
from jax import lax
from jax.experimental import pallas as pl
from jax.experimental.pallas import tpu as pltpu
from jax.sharding import PartitionSpec as P

MESH = pl.DeviceIdType.MESH
F32 = jnp.float32
BF16 = jnp.bfloat16
GROUPS = 4
INNER = 8
CHIPS = 16
RING = 4
TILE = 256
DH = 128
PIECE = DH // INNER
BATCHES = ((0, 4), (4, 8), (8, 11), (11, 16))


def dot(a, b, ca=1, cb=0):
    return lax.dot_general(a, b, (((ca,), (cb,)), ((), ())), preferred_element_type=F32)


def kernel(
    q_hbm, k_hbm, v_hbm, ld_hbm, ow_hbm, og_hbm,
    att_ref, qg_ref, kg_ref, vg_ref, wg_ref,
    q_ref, k_ref, v_ref, ld_ref, ow_ref,
    full, run_col, run_row, qgrow, qgt, ktail, vtail, weights, decay, masked, mixed, scale, mg, hgrad,
    kacc, vacc, upd, got, tots, gsum, gown, fswap, gtot, inc_out, inc,
    bupd, bgot, bsum, bown, swap, out_out, outg, dwl, dwb, dwp, dwo, dwq, dws, dwin,
    l_s, g_s, g_r, t_s, t_r, r1_s, r1_r, r2_s, r2_r, r2t_s, r2t_r, r3_s, r3_r, f_s, f_r,
    b1_s, b1_r, b2_s, b2_r, b3_s, b3_r, s_s, s_r, p_s, p_r, q_s, q_r, w_s, w_r, heard,
):
    tokens = q_ref.shape[0]
    half, quarter = tokens // 2, tokens // 4
    s = lax.axis_index("seq")
    h = lax.axis_index("head")
    g, j = s // INNER, s % INNER
    z, core = s // 2, s % 2
    y, x = h // RING, h % RING

    def head_at(dy, dx):
        return ((y + dy + RING) % RING) * RING + (x + dx + RING) % RING

    inner_peers = [(j + k) % INNER for k in range(1, INNER)]

    gsum[...] = jnp.zeros_like(gsum)
    bsum[...] = jnp.zeros_like(bsum)

    barrier = pltpu.get_barrier_semaphore()
    for seq, head in (
        (s, head_at(0, 1)), (s, head_at(0, -1)), (s, head_at(1, 0)), (s, head_at(-1, 0)), (2 * z + 1 - core, h),
        (2 * ((z + 1) % CHIPS) + core, h), (2 * ((z + CHIPS - 1) % CHIPS) + core, h),
    ):
        pl.semaphore_signal(barrier, inc=1, device_id=(seq, head), device_id_type=MESH)

    def tell(n):
        for sign in (1, -1):
            there = 2 * ((z + CHIPS + sign * 2**n) % CHIPS) + core
            pl.semaphore_signal(heard.at[n], inc=1, device_id=(there, h), device_id_type=MESH)

    def hear(n):
        pl.semaphore_wait(heard.at[n], 2)

    loads = [
        pltpu.make_async_copy(src, dst, l_s.at[n])
        for n, (src, dst) in enumerate(
            ((ld_hbm, ld_ref), (k_hbm, k_ref), (v_hbm, v_ref), (q_hbm, q_ref), (og_hbm, full.at[h]), (ow_hbm, ow_ref))
        )
    ]
    for copy in loads:
        copy.start()

    pl.semaphore_wait(barrier, 7)
    tell(0)

    started = []

    def remote(src, dst, send_sem, recv_sem, seq, head):
        return pltpu.make_async_remote_copy(
            src_ref=src, dst_ref=dst, send_sem=send_sem, recv_sem=recv_sem,
            device_id=(seq, head), device_id_type=MESH,
        )

    def begin(copy, when=None):
        if when is None:
            copy.start()
        else:
            pl.when(when)(copy.start)
            started.append((copy, when))

    def bytes_of(ref, send_sem, recv_sem):
        return remote(ref, ref, send_sem, recv_sem, s, h)

    def spread(src, dst, send_sem, recv_sem, sign):
        out = []
        for k in (2, 1, 3):
            p = g + sign * k
            inside = jnp.logical_and(p >= 0, p < GROUPS)
            for m in range(RING):
                there = (p + GROUPS) % GROUPS * INNER + (j + 2 * m) % INNER
                copy = remote(src, dst.at[g, j // 2], send_sem.at[k - 1], recv_sem.at[k - 1], there, h)
                pl.when(inside)(copy.start)
            every = bytes_of(dst.at[0], send_sem.at[k - 1], recv_sem.at[k - 1])
            started.append((every, inside))
            out.append((every, jnp.logical_and(g - sign * k >= 0, g - sign * k < GROUPS)))
        return out

    def exchange(buffer, send_sem, recv_sem):
        copy = remote(buffer.at[core], buffer.at[core], send_sem, recv_sem, 2 * z + 1 - core, h)
        begin(copy)
        started.append((copy, None))
        return copy

    def stacked(buffer):
        return jnp.concatenate([buffer[n % 2, n // 2] for n in range(INNER)], axis=0)

    def land(copies):
        for copy, when in copies:
            if when is None:
                copy.wait_recv()
            else:
                pl.when(when)(copy.wait_recv)

    def drain(copies):
        for copy, when in copies:
            if when is None:
                copy.wait_send()
            else:
                pl.when(when)(copy.wait_send)

    def to_inner(src, dst, send_sem, recv_sem):
        for p in inner_peers:
            piece = dst.at[j] if src is None else src.at[p]
            begin(remote(piece, dst.at[j], send_sem, recv_sem, g * INNER + p, h))
        every = bytes_of(dst.at[pl.ds(0, INNER - 1)], send_sem, recv_sem)
        started.append((every, None))
        return [(every, None)]

    def to_outer(dst, send_sem, recv_sem):
        for k in range(1, GROUPS):
            begin(remote(dst.at[g], dst.at[g], send_sem, recv_sem, (g + k) % GROUPS * INNER + j, h))
        every = bytes_of(dst.at[pl.ds(0, GROUPS - 1)], send_sem, recv_sem)
        started.append((every, None))
        return [(every, None)]

    gather = {}
    base = {"A": 0, "B": half}

    def step(kind, first, second):
        return (second, first) if kind == "A" else (first, second)

    def send(group, block, first, count, dy, dx, src=None):
        n = gather.setdefault(group, len(gather))
        part = full.at[block, pl.ds(first, count)]
        begin(remote(part if src is None else src.at[pl.ds(first, count)], part, g_s, g_r.at[n], s, head_at(dy, dx)))

    def arrived(group, blocks):
        rows = blocks if blocks is not None else full.at[0, pl.ds(0, half)]
        bytes_of(rows, g_s, g_r.at[gather[group]]).wait_recv()

    def far_group(kind, axis, off):
        if axis == 0:
            return ("first", kind)
        return ("middle",) if off == 0 else ("last", abs(off))

    def block_of(kind, first, second):
        return head_at(*step(kind, first, second))

    def along(kind, axis, sign):
        return step(kind, sign, 0) if axis == 0 else step(kind, 0, sign)

    def quarters(kind, axis, off, sign, block, src=None):
        part, late = (0, quarter) if sign == 1 else (quarter, 0)
        way = along(kind, axis, sign)
        send((kind, axis, off), block, base[kind] + part, quarter, *way, src=src)
        if axis == 0:
            group = ("rest", 0)
        else:
            group = ("rest", 1) if off != 2 else ("rest", 2)
        send(group, block, base[kind] + late, quarter, *way, src=src)

    def own(kind, axis):
        for sign in (1, -1):
            quarters(kind, axis, 0, sign, h, og_hbm)

    def relay(kind, axis, off):
        arrived((kind, axis, off), None)
        for sign in (1, -1):
            block = block_of(kind, -sign, 0) if axis == 0 else block_of(kind, off, -sign)
            part = base[kind] + (0 if sign == 1 else quarter)
            send(far_group(kind, axis, off), block, part, quarter, *along(kind, axis, sign))

    def turn(kind, off):
        for sign in (1, -1):
            quarters(kind, 1, off, sign, block_of(kind, off, 0))

    own("A", 0)
    own("B", 0)
    own("B", 1)
    own("A", 1)

    lane = lax.broadcasted_iota(jnp.int32, (DH, DH), 1)
    row = lax.broadcasted_iota(jnp.int32, (DH, DH), 0)
    lower = lane <= row
    offset = jnp.zeros((1, 1), F32)
    loads[0].wait()
    for n in range(tokens // DH):
        piece = jnp.broadcast_to(ld_ref[:, n * DH : (n + 1) * DH], (DH, DH))
        col = jnp.sum(jnp.where(lower, piece, 0.0), axis=1, keepdims=True) + offset
        offset = col[DH - 1 : DH, :]
        wide = jnp.broadcast_to(col, (DH, DH))
        run_col[n * DH : (n + 1) * DH, :] = wide
        run_row[:, n * DH : (n + 1) * DH] = wide.T[0:8, :]
    total = jnp.broadcast_to(offset, (1, DH))
    tots[j] = total

    hear(0)
    tell(1)

    rc = run_col[...]
    tail = jnp.exp(total - rc)
    loads[1].wait()
    loads[2].wait()
    kt = (k_ref[...].astype(F32) * tail).astype(BF16)
    ktail[...] = kt
    upd[...] = dot(kt, v_ref[...], 0, 0).astype(BF16).reshape(INNER, PIECE, DH)
    got[j] = upd[j]
    vtail[...] = (v_ref[...].astype(F32) * tail).astype(BF16)
    loads[3].wait()
    qgrow[...] = (q_ref[...].astype(F32) * jnp.exp(rc)).astype(BF16)
    loads[4].wait()
    loads[5].wait()

    trow = lax.broadcasted_iota(jnp.int32, (TILE, TILE), 0)
    tcol = lax.broadcasted_iota(jnp.int32, (TILE, TILE), 1)
    causal = trow >= tcol
    def local(t):
        here = slice(t * TILE, (t + 1) * TILE)
        q = q_ref[here, :]
        here_run = run_col[here, 0:1]
        for u in range(t + 1):
            there = slice(u * TILE, (u + 1) * TILE)
            spread = here_run - run_row[0:1, there]
            if u == t:
                fade = jnp.where(causal, jnp.exp(jnp.where(causal, spread, 0.0)), 0.0)
            else:
                fade = jnp.exp(spread)
            decay[here, there] = fade
            score = dot(q, k_ref[there, :], 1, 1)
            weights[here, there] = (score * fade).astype(BF16)
        n = (t + 1) * TILE
        mixed[here, :] = dot(weights[here, :n], v_ref[:n, :])

    local(0)
    local(1)
    hear(1)
    tell(2)
    totals_in = to_inner(None, tots, t_s, t_r)
    round1 = to_inner(upd, got, r1_s, r1_r)
    local(2)
    local(3)

    relay("A", 0, 0)
    relay("B", 0, 0)
    arrived(("rest", 0), full.at[0])
    for off in (-1, 1):
        turn("A", off)
        turn("B", off)

    land(totals_in)
    tot = [tots[n] for n in range(INNER)]
    grow = [jnp.exp(t) for t in tot]
    everything = tot[0]
    for n in range(1, INNER):
        everything = everything + tot[n]
    gtot[g] = everything
    hear(2)
    round2t = to_outer(gtot, r2t_s, r2t_r)
    land(round1)
    state = jnp.zeros((PIECE, DH), F32)
    before = []
    for n in range(INNER):
        before.append(state)
        state = grow[n] * state + got[n].astype(F32)
    gown[...] = state.astype(BF16)
    round2 = spread(gown, gsum, r2_s, r2_r, 1)
    for n in range(INNER):
        inc_out[n] = before[n].astype(BF16)
    inc[j] = inc_out[j]
    round3 = to_inner(inc_out, inc, r3_s, r3_r)

    relay("A", 1, 0)
    relay("B", 1, 0)
    arrived(("first", "A"), None)
    turn("A", 2)
    arrived(("first", "B"), None)
    turn("B", 2)

    def head_part(off, first):
        top, low = slice(0, half), slice(half, tokens)
        b = ((y + off + RING) % RING) * RING
        blocks = jnp.concatenate([full[b + n, top, :] for n in range(RING)], axis=1)
        part_a = dot(blocks, ow_ref[pl.ds(pl.multiple_of(b * DH, DH), RING * DH), :])
        b = (x + off + RING) % RING
        blocks = jnp.concatenate([full[b + RING * n, low, :] for n in range(RING)], axis=1)
        rows = [ow_ref[pl.ds(pl.multiple_of((b + RING * n) * DH, DH), DH), :] for n in range(RING)]
        part_b = dot(blocks, jnp.concatenate(rows, axis=0))
        if first:
            hgrad[top, :] = part_a
            hgrad[low, :] = part_b
        else:
            hgrad[top, :] = hgrad[top, :] + part_a
            hgrad[low, :] = hgrad[low, :] + part_b

    def head_rest(offsets):
        for rows, at in ((slice(0, half), lambda n: head_at(2, n)), (slice(half, tokens), lambda n: head_at(n, 2))):
            blocks = [full[at(n), rows, :] for n in offsets]
            wide = [ow_ref[pl.ds(pl.multiple_of(at(n) * DH, DH), DH), :] for n in offsets]
            if len(offsets) > 1:
                part = dot(jnp.concatenate(blocks, axis=1), jnp.concatenate(wide, axis=0))
            else:
                part = dot(blocks[0], wide[0])
            hgrad[rows, :] = hgrad[rows, :] + part

    head_part(0, True)

    land(round2t)
    land(round2)
    carried = jnp.zeros((RING, PIECE, DH), F32)
    for n in range(GROUPS):
        carried = jnp.where(n < g, jnp.exp(gtot[n])[None] * carried + gsum[n].astype(F32), carried)
    fswap[core] = carried
    swapped = exchange(fswap, f_s, f_r)

    for off in (-1, 1):
        relay("A", 1, off)
        relay("B", 1, off)

    land(round3)
    swapped.wait_recv()
    head = jnp.zeros((1, DH), F32)
    for n in range(INNER):
        head = head + jnp.where(n < j, tot[n], 0.0)
    incoming = (inc[...].reshape(DH, DH).astype(F32) + jnp.exp(head) * stacked(fswap)).astype(BF16)
    whole = mixed[...] + dot(qgrow[...], incoming)
    inv = lax.rsqrt(jnp.mean(whole * whole, axis=1, keepdims=True) + 1e-05)
    normed = whole * inv
    att = normed.astype(BF16)
    att_ref[...] = att
    mixed[...] = normed
    scale[...] = jnp.broadcast_to(inv, (tokens, DH))
    att_t = att.T
    qgt[...] = qgrow[...].T

    near = (0, -1, 1)
    order = [(a, b) for a in near for b in near]
    order += [(0, 2), (2, 0), (-1, 2), (2, -1), (1, 2), (2, 1), (2, 2)]
    blocks = [head_at(a, b) for a, b in order]
    pair_in = []
    other = z + 1 - 2 * (z % 2)

    def contribute(batch):
        lo, hi = BATCHES[batch]
        for n in range(lo, hi):
            rows = dot(att_t, full[blocks[n]]).T
            dwl[0, n] = rows[: DH // 2, :]
            dwl[1, n] = rows[DH // 2 :, :]
            dwb[n] = dwl[1 - core, n].astype(BF16)
        part = pl.ds(lo, hi - lo)
        copy = remote(dwb.at[part], dwp.at[part], p_s.at[batch], p_r.at[batch], 2 * z + 1 - core, h)
        begin(copy)
        started.append((copy, None))
        pair_in.append(copy)

    def ours(n):
        return blocks[n] % 2 != z % 2

    def across(n):
        return remote(dwo.at[n], dwq.at[n], q_s, q_r.at[n], 2 * other + core, h)

    def pair_up(batch):
        pair_in[batch].wait_recv()
        for n in range(*BATCHES[batch]):
            both = dwl[core, n] + dwp[n].astype(F32)
            dwl[core, n] = both
            dwo[n] = both.astype(BF16)
            pl.when(jnp.logical_not(ours(n)))(across(n).start)

    def deliver(batch):
        for n in range(*BATCHES[batch]):
            f = blocks[n]

            @pl.when(ours(n))
            def _():
                across(n).wait_recv()
                dws[n] = (dwl[core, n] + dwq[n].astype(F32)).astype(BF16)
                remote(dws.at[n], dwin.at[z // 2], w_s, w_r, 2 * f + core, h).start()

    arrived(("rest", 1), full.at[pl.ds(0, 3)])
    contribute(0)
    contribute(1)
    pair_up(0)
    arrived(("middle",), full.at[0])
    contribute(2)
    pair_up(1)
    relay("A", 1, 2)
    relay("B", 1, 2)
    pair_up(2)
    arrived(("rest", 2), full.at[0])
    deliver(0)
    head_part(-1, False)
    head_part(1, False)
    deliver(1)
    deliver(2)

    arrived(("last", 1), full.at[pl.ds(0, 2)])
    head_rest((0, -1, 1))
    arrived(("last", 2), full.at[0])

    head_rest((2,))
    normed = mixed[...]
    head_grad = hgrad[...]
    grad = (head_grad - normed * jnp.mean(head_grad * normed, axis=1, keepdims=True)) * scale[...]
    mgrad = grad.astype(BF16)
    mg[...] = mgrad
    bupd[...] = dot(qgt[...], mgrad).astype(BF16).reshape(INNER, PIECE, DH)
    bgot[j] = bupd[j]
    back1 = to_inner(bupd, bgot, b1_s, b1_r)

    att_t = att_ref[...].T
    contribute(3)
    for t in range(tokens // TILE):
        here = slice(t * TILE, (t + 1) * TILE)
        n = (t + 1) * TILE
        pair = dot(mg[here, :], v_ref[:n, :], 1, 1)
        masked[here, :n] = (pair * decay[here, :n]).astype(BF16)
        inside = dot(masked[here, :n], k_ref[:n, :])
        grown = (mg[here, :].astype(F32) * jnp.exp(run_col[here, :])).astype(BF16)
        qg_ref[here, :] = (inside + dot(grown, incoming, 1, 1)).astype(BF16)

    pair_up(3)

    land(back1)
    state = jnp.zeros((PIECE, DH), F32)
    after = [None] * INNER
    for n in reversed(range(INNER)):
        after[n] = state
        state = bgot[n].astype(F32) + grow[n] * state
    bown[...] = state.astype(BF16)
    back2 = spread(bown, bsum, b2_s, b2_r, -1)
    for n in range(INNER):
        out_out[n] = after[n].astype(BF16)
    outg[j] = out_out[j]
    back3 = to_inner(out_out, outg, b3_s, b3_r)

    deliver(3)
    for u in range(tokens // TILE):
        there = slice(u * TILE, (u + 1) * TILE)
        m = u * TILE
        kacc[there, :] = dot(masked[m:, there], q_ref[m:, :], 0, 0)
        vacc[there, :] = dot(weights[m:, there], mg[m:, :], 0, 0)

    drain(started[:-4])
    del started[:-4]
    bytes_of(full.at[pl.ds(0, RING * RING - 1)], g_s, g_r.at[0]).wait_send()

    land(back2)
    trail = jnp.zeros((1, DH), F32)
    for n in range(INNER):
        trail = trail + jnp.where(n > j, tot[n], 0.0)
    carried = jnp.zeros((RING, PIECE, DH), F32)
    for n in reversed(range(GROUPS)):
        carried = jnp.where(n > g, bsum[n].astype(F32) + jnp.exp(gtot[n])[None] * carried, carried)
    swap[core] = carried
    swapped = exchange(swap, s_s, s_r)
    land(back3)
    swapped.wait_recv()
    outgoing = (outg[...].reshape(DH, DH).astype(F32) + jnp.exp(trail) * stacked(swap)).astype(BF16)
    kg_ref[...] = (kacc[...] + dot(vtail[...], outgoing, 1, 1)).astype(BF16)
    vg_ref[...] = (vacc[...] + dot(ktail[...], outgoing)).astype(BF16)

    weights_in = bytes_of(dwin, w_s, w_r)
    weights_in.wait_recv()
    acc = dwin[0].astype(F32)
    for n in range(1, CHIPS // 2):
        acc = acc + dwin[n].astype(F32)
    wg_ref[...] = acc.astype(BF16)

    weights_in.wait_send()
    bytes_of(dwo.at[pl.ds(0, CHIPS // 2)], q_s, q_r.at[0]).wait_send()
    drain(started)


def hand_out(*refs):
    n = len(refs) // 2
    sem = refs[-1]
    copies = [pltpu.make_async_copy(refs[i], refs[n + i], sem.at[i]) for i in range(n)]
    for copy in copies:
        copy.start()
    for copy in copies:
        copy.wait()


def on_device(queries, keys, values, log_decay, out_weight, out_grad):
    tokens = queries.shape[0]
    vmem = pl.BlockSpec(memory_space=pltpu.VMEM)
    anywhere = pl.BlockSpec(memory_space=pl.ANY)
    rows = out_weight.shape[0] // (GROUPS * INNER)
    shapes = ((tokens, DH),) * 4 + ((rows, DH),)
    dma = pltpu.SemaphoreType.DMA
    inner, outer = dma, dma((GROUPS - 1,))
    blocks = RING * RING
    scratch = [
        *[pltpu.VMEM((tokens, DH), BF16)] * 3,
        pltpu.VMEM((1, tokens), F32),
        pltpu.VMEM(out_weight.shape, BF16),
        pltpu.VMEM((blocks, tokens, DH), BF16),
        pltpu.VMEM((tokens, DH), F32),
        pltpu.VMEM((8, tokens), F32),
        pltpu.VMEM((tokens, DH), BF16),
        pltpu.VMEM((DH, tokens), BF16),
        *[pltpu.VMEM((tokens, DH), BF16)] * 2,
        pltpu.VMEM((tokens, tokens), BF16),
        pltpu.VMEM((tokens, tokens), F32),
        pltpu.VMEM((tokens, tokens), BF16),
        *[pltpu.VMEM((tokens, DH), F32)] * 2,
        pltpu.VMEM((tokens, DH), BF16),
        *[pltpu.VMEM((tokens, DH), F32)] * 3,
        *[pltpu.VMEM((INNER, PIECE, DH), BF16)] * 2,
        pltpu.VMEM((INNER, 1, DH), F32),
        pltpu.VMEM((GROUPS, RING, PIECE, DH), BF16),
        pltpu.VMEM((PIECE, DH), BF16),
        pltpu.VMEM((2, RING, PIECE, DH), F32),
        pltpu.VMEM((GROUPS, 1, DH), F32),
        *[pltpu.VMEM((INNER, PIECE, DH), BF16)] * 4,
        pltpu.VMEM((GROUPS, RING, PIECE, DH), BF16),
        pltpu.VMEM((PIECE, DH), BF16),
        pltpu.VMEM((2, RING, PIECE, DH), F32),
        *[pltpu.VMEM((INNER, PIECE, DH), BF16)] * 2,
        pltpu.VMEM((2, blocks, rows, DH), F32),
        *[pltpu.VMEM((blocks, rows, DH), BF16)] * 5,
        pltpu.VMEM((CHIPS // 2, rows, DH), BF16),
        dma((6,)),
        dma, dma((18,)),
        inner, inner,
        inner, inner, outer, outer, dma, dma, inner, inner, dma, dma,
        inner, inner, outer, outer, inner, inner, dma, dma,
        dma((len(BATCHES),)), dma((len(BATCHES),)), dma, dma((blocks,)), dma, dma,
        pltpu.SemaphoreType.REGULAR((3,)),
    ]
    results = pl.pallas_call(
        kernel,
        out_shape=tuple(pltpu.VMEM(shape, BF16) for shape in shapes),
        in_specs=[anywhere] * 6,
        out_specs=(vmem,) * 5,
        scratch_shapes=scratch,
        compiler_params=pltpu.CompilerParams(collective_id=0, has_side_effects=True),
    )(queries, keys, values, log_decay, out_weight, out_grad)
    return pl.pallas_call(
        hand_out,
        out_shape=tuple(jax.ShapeDtypeStruct(shape, BF16) for shape in shapes),
        in_specs=[vmem] * 5,
        out_specs=(anywhere,) * 5,
        scratch_shapes=[dma((5,))],
    )(*[pltpu.with_memory_space_constraint(array, pltpu.VMEM) for array in results])


def solution(mesh):
    return jax.shard_map(
        on_device,
        mesh=mesh,
        in_specs=(
            P("seq", "head"),
            P("seq", "head"),
            P("seq", "head"),
            P("head", "seq"),
            P(None, "head"),
            P("seq", "head"),
        ),
        out_specs=(P("seq", "head"),) * 5,
        check_vma=False,
    )
```
